32 devices in a mesh: section: 2 (over y), batch: 4 (over x, core), tensor: 4 (over z).
Axes of the slice: x: 2, y: 2, z: 4, core: 2. Of those that a mesh axis runs over, the one named last changes fastest.
Arguments:
- ids_beam: int32 [8, 256], P('batch'), may hold values from 0 to 15999
- beam_map: int32 [8], replicated, may hold values from 0 to 7, each once
- lengths: int32 [8], replicated, may hold values from 1 to 256, 1536 in all
- embed_table: bfloat16 [16000, 4096], P(None, ('section', 'tensor')), may hold values from -6 to 6
- gain_attn: bfloat16 [2, 4096], P('section'), may hold values from 0.099609375 to 1.8984375
- w_query: bfloat16 [2, 4096, 4096], P('section', None, 'tensor'), may hold values from -1 to 1
- w_key: bfloat16 [2, 4096, 4096], P('section', None, 'tensor'), may hold values from -3 to 3
- w_value: bfloat16 [2, 4096, 4096], P('section', None, 'tensor'), may hold values from -0.09375 to 0.09375
- w_out: bfloat16 [2, 4096, 4096], P('section', 'tensor'), may hold values from -0.09375 to 0.09375
- gain_mlp: bfloat16 [2, 4096], P('section'), may hold values from 0.099609375 to 1.8984375
- w_gate: bfloat16 [2, 4096, 8192], P('section', None, 'tensor'), may hold values from -0.09375 to 0.09375
- w_up: bfloat16 [2, 4096, 8192], P('section', None, 'tensor'), may hold values from -0.09375 to 0.09375
- w_down: bfloat16 [2, 8192, 4096], P('section', 'tensor'), may hold values from -0.0625 to 0.0625
- final_gain: bfloat16 [4096], replicated, may hold values from 0.099609375 to 1.8984375
- score_weight: bfloat16 [4096], replicated, may hold values from -0.09375 to 0.09375
Outputs:
- residual_output: bfloat16 [8, 256, 4096], P('batch', 'tensor', 'section')
- scores: float32 [8], P('batch')
The draws below stay inside these ranges and needn't reach their ends.
Inputs may be any that keep to these rules, and one draw needn't show every extreme that they name: A permutation: candidate c reads row beam_map[c] of ids_beam. `lengths`: the score is read at the last token before the padding.
All inputs are finite; a program needn't handle non-finite values.
Results may differ from the reference program's by a relative error of at most 0.04.
Values may be sent and summed in bfloat16 or wider, within the bound.
No kernel may reach another device: no remote copies, remote signals or barrier semaphores. Data moves between devices by JAX's collectives and lax.ppermute only.
A program may use at most 256 MiB of HBM per device.

```python
import math
import jax
import jax.numpy as jnp
import numpy as np
from jax import lax

D = 4096
HEADS = 32
HEAD_DIM = 128
FFW = 8192
VOCAB = 16000
LEN = 256
LAYERS = 2
CANDS = 8
N_TENSOR = 4


def shared_normal(key, salt_value):
    return jnp.clip(jax.random.normal(jax.random.fold_in(key, salt_value), (LAYERS, D, D), jnp.float32), -6.0, 6.0)


def draw_w_query(key, part):
    values = shared_normal(key, 11) * D ** (-0.5)
    return jnp.clip(values, -1.0, 1.0).astype(jnp.bfloat16)


def draw_w_key(key, part):
    unrelated = shared_normal(key, 12) * D ** (-0.5)
    values = unrelated
    return jnp.clip(values, -3.0, 3.0).astype(jnp.bfloat16)


def place_ends(result, own_key, smallest, largest):
    index_at = [jax.random.randint(jax.random.fold_in(own_key, axis), (), 0, length) for axis, length in enumerate(result.shape)]
    longest = result.shape.index(max(result.shape))
    next_to = index_at[:longest] + [(index_at[longest] + 1) % result.shape[longest]] + index_at[longest + 1:]
    return result.at[tuple(index_at)].set(smallest).at[tuple(next_to)].set(largest)


def steps_of(own_key, extent, split, low, top_value):
    loudness = 1.0
    for dim, parts in split:
        steps = jax.random.uniform(jax.random.fold_in(jax.random.fold_in(own_key, 6), dim), (parts,), jnp.float32, low / len(split), top_value / len(split))
        loudness = loudness * jnp.repeat(jnp.exp(steps), extent[dim] // parts).reshape((-1,) + (1,) * (len(extent) - 1 - dim))
    return loudness


def rank_bounds(number_of, lean):
    weights = [(1 << 20) // math.isqrt(standing ** lean) + 1 for standing in range(1, number_of + 1)]
    scale = 1 + sum(weights) // (1 << 30)
    return np.cumsum(np.array([max(1, weight // scale) for weight in weights]))


def ranked_ids(key, extent, number_of, skew):
    listing = rank_bounds(number_of, skew)
    pick = jax.random.randint(jax.random.fold_in(key, 1), extent, 0, int(listing[number_of - 1]))
    grade = jnp.searchsorted(jnp.asarray(listing, jnp.int32), pick, side="right")
    return jax.random.permutation(jax.random.fold_in(key, 2), number_of)[grade].astype(jnp.int32)


def split_up(count, total, most, slope):
    weights = [(1 << 20) // math.isqrt(grade ** slope) + 1 for grade in range(2, count + 1)]
    surplus, given = total - most - (count - 1), [1] * (count - 1)
    while surplus > 0:
        free = [i for i in range(count - 1) if given[i] < most]
        whole, remaining = sum([weights[i] for i in free]), surplus
        for i in free:
            addition = min(most - given[i], max(1, remaining * weights[i] // whole), surplus)
            given[i] = given[i] + addition
            surplus = surplus - addition
    return np.array([most] + given)


def ragged(key, number_of, total, most, slope):
    if number_of == 2:
        one = jax.random.randint(key, (), max(1, total - most), min(most, total - 1) + 1)
        return jnp.stack([one, total - one])
    sizes = jnp.asarray(split_up(number_of, total, most, slope), jnp.int32)
    pairs = (number_of - 1) // 2
    donor, receiver = sizes[1:1 + 2 * pairs:2], sizes[2:2 + 2 * pairs:2]
    room = jnp.minimum(donor - 1, most - receiver)
    moved = jax.random.randint(jax.random.fold_in(key, 1), (pairs,), 0, 1 << 20) % (room + 1)
    sizes = sizes.at[1:1 + 2 * pairs:2].set(donor - moved).at[2:2 + 2 * pairs:2].set(receiver + moved)
    return sizes[jax.random.permutation(jax.random.fold_in(key, 2), number_of)]


def normal_values(key, extent, spread, reach, pieces=(), kind=jnp.bfloat16):
    gain = steps_of(key, extent, pieces, -0.22, 0.18) if pieces else 1.0
    values = jax.random.normal(key, extent, jnp.float32) * spread * gain
    return jnp.minimum(jnp.maximum(values, -reach), reach).astype(kind)


def setup_inputs(seed: int = 0) -> dict:
    splits = jax.random.split(jax.random.key(seed), 16)
    return {
        "ids_beam": place_ends(ranked_ids(splits[0], (CANDS, LEN), VOCAB, 2), jax.random.fold_in(splits[0], 3), 0, VOCAB - 1).astype(jnp.int32),
        "beam_map": jax.random.permutation(splits[1], CANDS).astype(jnp.int32),
        "lengths": ragged(splits[2], CANDS, CANDS * LEN * 3 // 4, LEN, 0).astype(jnp.int32),
        "embed_table": normal_values(splits[3], (VOCAB, D), 1.0, 6.0, ((1, 8),)),
        "gain_attn": jnp.clip(1.0 + 0.18 * jax.random.normal(splits[4], (LAYERS, D), jnp.float32), 0.099609375, 1.8984375).astype(jnp.bfloat16),
        "w_query": draw_w_query(jax.random.fold_in(splits[15], 71), 0),
        "w_key": draw_w_key(jax.random.fold_in(splits[15], 71), 0),
        "w_value": normal_values(splits[7], (LAYERS, D, D), D ** -0.5, 0.09375, ((0, 2), (2, 4))),
        "w_out": normal_values(splits[8], (LAYERS, D, D), D ** -0.5, 0.09375, ((0, 2), (1, 4))),
        "gain_mlp": jnp.clip(1.0 + 0.18 * jax.random.normal(splits[9], (LAYERS, D), jnp.float32), 0.099609375, 1.8984375).astype(jnp.bfloat16),
        "w_gate": normal_values(splits[10], (LAYERS, D, FFW), D ** -0.5, 0.09375, ((0, 2), (2, 4))),
        "w_up": normal_values(splits[11], (LAYERS, D, FFW), D ** -0.5, 0.09375, ((0, 2), (2, 4))),
        "w_down": normal_values(splits[12], (LAYERS, FFW, D), FFW ** -0.5, 0.0625, ((0, 2), (1, 4))),
        "final_gain": jnp.clip(1.0 + 0.18 * jax.random.normal(splits[13], (D,), jnp.float32), 0.099609375, 1.8984375).astype(jnp.bfloat16),
        "score_weight": normal_values(splits[14], (D,), D ** -0.5, 0.09375),
    }


EPSILON = 1e-05
ROTARY_FREQ_BASE = 10000.0

def rms_norm(hidden, scale_gain):
    values = hidden.astype(jnp.float32)
    inverse = lax.rsqrt(lax.optimization_barrier(jnp.mean(values * values, axis=-1, keepdims=True)) + EPSILON)
    return (values * inverse * scale_gain.astype(jnp.float32)).astype(jnp.bfloat16)

def rope_tables(length, head_dim):
    half_dim = head_dim // 2
    frequency = ROTARY_FREQ_BASE ** (-(jnp.arange(half_dim, dtype=jnp.float32) / half_dim))
    angles = jnp.arange(length, dtype=jnp.float32)[:, None] * frequency[None, :]
    return (jnp.cos(angles), jnp.sin(angles))

def rotate(values, cosine_table, sine_table):
    half_dim = values.shape[-1] // 2
    first_half = values[..., :half_dim]
    second_half = values[..., half_dim:]
    cosine_wide = cosine_table[:, None, :]
    sine_wide = sine_table[:, None, :]
    return jnp.concatenate([first_half * cosine_wide - second_half * sine_wide, second_half * cosine_wide + first_half * sine_wide], axis=-1)

def shard_sum(left_rows, right_cols, shards):
    length = left_rows.shape[0]
    width = left_rows.shape[1] // shards
    left_pieces = left_rows.reshape(length, shards, width).astype(jnp.float32)
    right_pieces = right_cols.reshape(shards, width, right_cols.shape[1]).astype(jnp.float32)
    partial_sums = jnp.einsum('wgy,gye->gwe', left_pieces, right_pieces)
    rounded = lax.optimization_barrier(partial_sums.astype(jnp.bfloat16))
    return lax.optimization_barrier(jnp.sum(rounded.astype(jnp.float32), axis=0))

def decoder_layer(hidden, layer_weights, cosine_table, sine_table, causal):
    gain_attn, w_query, w_key, w_value, w_out, gain_mlp, w_gate, w_up, w_down = layer_weights
    length = hidden.shape[0]
    normed = rms_norm(hidden, gain_attn)
    query_proj = jnp.dot(normed, w_query, preferred_element_type=jnp.float32).reshape(length, HEADS, HEAD_DIM)
    key_proj = jnp.dot(normed, w_key, preferred_element_type=jnp.float32).reshape(length, HEADS, HEAD_DIM)
    value_proj = jnp.dot(normed, w_value, preferred_element_type=jnp.float32).astype(jnp.bfloat16).reshape(length, HEADS, HEAD_DIM)
    query_rot = rotate(query_proj, cosine_table, sine_table).astype(jnp.bfloat16)
    key_rot = rotate(key_proj, cosine_table, sine_table).astype(jnp.bfloat16)
    scores = jnp.einsum('qhd,khd->hqk', query_rot.astype(jnp.float32), key_rot.astype(jnp.float32)) * HEAD_DIM ** (-0.5)
    scores = jnp.where(causal[None], scores, -jnp.inf)
    weights_soft = jax.nn.softmax(scores, axis=-1).astype(jnp.bfloat16)
    attended = jnp.einsum('hqk,khd->qhd', weights_soft.astype(jnp.float32), value_proj.astype(jnp.float32))
    attended = attended.astype(jnp.bfloat16).reshape(length, HEADS * HEAD_DIM)
    attn_sum = shard_sum(attended, w_out, N_TENSOR)
    middle = (hidden.astype(jnp.float32) + attn_sum).astype(jnp.bfloat16)
    normed_mlp = rms_norm(middle, gain_mlp)
    gate_proj = jnp.dot(normed_mlp, w_gate, preferred_element_type=jnp.float32)
    up_proj = jnp.dot(normed_mlp, w_up, preferred_element_type=jnp.float32)
    inner_act = (jax.nn.silu(gate_proj) * up_proj).astype(jnp.bfloat16)
    mlp_sum = shard_sum(inner_act, w_down, N_TENSOR)
    return (middle.astype(jnp.float32) + mlp_sum).astype(jnp.bfloat16)

def final_score(last_row, final_gain, score_weight):
    values = last_row.astype(jnp.float32)
    inverse = lax.rsqrt(lax.optimization_barrier(jnp.mean(values * values, axis=-1, keepdims=True)) + EPSILON)
    return lax.optimization_barrier(jnp.sum(values * inverse * final_gain.astype(jnp.float32) * score_weight.astype(jnp.float32), axis=-1))

def reference(ids_beam, beam_map, lengths, embed_table, gain_attn, w_query, w_key, w_value, w_out, gain_mlp, w_gate, w_up, w_down, final_gain, score_weight):
    cosine_table, sine_table = rope_tables(LEN, HEAD_DIM)
    token_positions = jnp.arange(LEN)
    causal = token_positions[:, None] >= token_positions[None, :]
    stacked = (gain_attn, w_query, w_key, w_value, w_out, gain_mlp, w_gate, w_up, w_down)
    layers = [tuple((tensor_arg[layer_index] for tensor_arg in stacked)) for layer_index in range(LAYERS)]

    def one_candidate(cand_index):
        beam_row = beam_map[cand_index]
        tokens = lax.dynamic_index_in_dim(ids_beam, beam_row, 0, keepdims=False)
        hidden = embed_table[tokens]
        for layer_weights in layers:
            hidden = decoder_layer(hidden, layer_weights, cosine_table, sine_table, causal)
        last_pos = (lengths[cand_index] - 1).astype(jnp.int32)
        last_row = lax.dynamic_index_in_dim(hidden, last_pos, 0, keepdims=False)
        return (hidden, final_score(last_row, final_gain, score_weight))
    residual_output, scores = lax.map(one_candidate, jnp.arange(CANDS, dtype=jnp.int32))
    return (residual_output, scores)
```

```python
import functools

import jax
import jax.numpy as jnp
import numpy as np
from jax import lax
from jax.experimental import pallas as pl
from jax.experimental.pallas import tpu as pltpu
from jax.sharding import PartitionSpec as P

HEAD_DIM = 128
EPSILON = 1e-05
ROTARY_FREQ_BASE = 10000.0
BOTH = ("section", "tensor")
WIDE = 256
VMEM_LIMIT = 50 * 2**20


def rms_norm(hidden, scale_gain):
    values = hidden.astype(jnp.float32)
    inverse = lax.rsqrt(jnp.mean(values * values, axis=-1, keepdims=True) + EPSILON)
    return (values * inverse * scale_gain.astype(jnp.float32)).astype(jnp.bfloat16)


def rope_tables(length):
    half_dim = HEAD_DIM // 2
    frequency = ROTARY_FREQ_BASE ** (-(np.arange(half_dim, dtype=np.float64) / half_dim))
    angles = np.arange(length, dtype=np.float64)[:, None] * frequency[None, :]
    cosine, sine = np.cos(angles), np.sin(angles)
    cosine = np.concatenate([cosine, cosine], axis=1).astype(np.float32)
    sine = np.concatenate([-sine, sine], axis=1).astype(np.float32)
    return cosine, sine


def dot(left, right):
    return jnp.dot(left, right, preferred_element_type=jnp.float32)


def split_refs(refs, pieces):
    return refs[:pieces], refs[pieces : 2 * pieces], refs[2 * pieces :]


def attention_kernel(pieces, cos_ref, sin_ref, row_ref, col_ref, wq_ref, wk_ref, wv_ref, wo_ref, *refs):
    x_refs, out_refs, (x_all, total) = split_refs(refs, pieces)
    step = pl.program_id(0)
    share = x_refs[0].shape[0]

    @pl.when(step == 0)
    def _():
        for j in range(pieces):
            x_all[j * share : (j + 1) * share, :] = x_refs[j][...]

    x = x_all[...]
    cosine, sine = cos_ref[...], sin_ref[...]
    visible = row_ref[...] >= col_ref[...]
    query, key, value = dot(x, wq_ref[0]), dot(x, wk_ref[0]), dot(x, wv_ref[0])
    value = value.astype(jnp.bfloat16)
    outs = []
    for head in range(query.shape[1] // HEAD_DIM):
        cut = slice(head * HEAD_DIM, (head + 1) * HEAD_DIM)
        q, k, v = query[:, cut], key[:, cut], value[:, cut]
        q = (q * cosine + pltpu.roll(q, HEAD_DIM // 2, 1) * sine).astype(jnp.bfloat16)
        k = (k * cosine + pltpu.roll(k, HEAD_DIM // 2, 1) * sine).astype(jnp.bfloat16)
        scores = lax.dot_general(
            q, k, (((1,), (1,)), ((), ())), preferred_element_type=jnp.float32
        ) * HEAD_DIM ** (-0.5)
        scores = jnp.where(visible, scores, -jnp.inf)
        scores = jnp.exp(scores - jnp.max(scores, axis=-1, keepdims=True))
        probs = scores / jnp.sum(scores, axis=-1, keepdims=True)
        outs.append(dot(probs.astype(jnp.bfloat16), v).astype(jnp.bfloat16))
    part = dot(jnp.concatenate(outs, axis=1), wo_ref[0])

    @pl.when(step == 0)
    def _():
        total[...] = part

    @pl.when(step > 0)
    def _():
        total[...] += part

    @pl.when(step == pl.num_programs(0) - 1)
    def _():
        for j in range(pieces):
            out_refs[j][...] = total[j * share : (j + 1) * share, :].astype(jnp.bfloat16)


def mlp_kernel(pieces, wg_ref, wu_ref, wd_ref, *refs):
    x_refs, out_refs, (x_all, total) = split_refs(refs, pieces)
    step = pl.program_id(0)
    share = x_refs[0].shape[0]

    @pl.when(step == 0)
    def _():
        for j in range(pieces):
            x_all[j * share : (j + 1) * share, :] = x_refs[j][...]

    x = x_all[...]
    gate, up = dot(x, wg_ref[0]), dot(x, wu_ref[0])
    inner = (gate / (1.0 + jnp.exp(-gate)) * up).astype(jnp.bfloat16)
    part = dot(inner, wd_ref[0])

    @pl.when(step == 0)
    def _():
        total[...] = part

    @pl.when(step > 0)
    def _():
        total[...] += part

    @pl.when(step == pl.num_programs(0) - 1)
    def _():
        for j in range(pieces):
            out_refs[j][...] = total[j * share : (j + 1) * share, :].astype(jnp.bfloat16)


def whole(array):
    return pl.BlockSpec(array.shape, lambda i: (0,) * array.ndim)


def fused(kernel, name, tables, by_columns, by_rows, pieces):
    share, width = pieces[0].shape
    length = share * len(pieces)
    hidden = by_rows.shape[1]
    wide = min(WIDE, hidden)
    weights = list(by_columns) + [by_rows]
    flops = 2 * length * sum(w.size for w in weights)
    traffic = 2 * sum(w.size for w in weights) + 4 * length * width
    return pl.pallas_call(
        functools.partial(kernel, len(pieces)),
        out_shape=[jax.ShapeDtypeStruct((share, width), jnp.bfloat16) for _ in pieces],
        grid=(hidden // wide,),
        in_specs=[whole(t) for t in tables]
        + [pl.BlockSpec((1, width, wide), lambda i: (0, 0, i)) for _ in by_columns]
        + [pl.BlockSpec((1, wide, width), lambda i: (0, i, 0))]
        + [whole(p) for p in pieces],
        out_specs=[pl.BlockSpec((share, width), lambda i: (0, 0)) for _ in pieces],
        scratch_shapes=[
            pltpu.VMEM((length, width), jnp.bfloat16),
            pltpu.VMEM((length, width), jnp.float32),
        ],
        compiler_params=pltpu.CompilerParams(
            dimension_semantics=("arbitrary",), vmem_limit_bytes=VMEM_LIMIT
        ),
        cost_estimate=pl.CostEstimate(flops=flops, bytes_accessed=traffic, transcendentals=0),
        name=name,
    )(*tables, *weights, *pieces)


def distances(count):
    return [1 << bit for bit in range(count.bit_length() - 1)]


def swap(value, distance):
    count = lax.axis_size("tensor")
    return lax.ppermute(value, "tensor", [(z, z ^ distance) for z in range(count)])


def gather_rows(own):
    count = lax.axis_size("tensor")
    got = {0: own}
    for distance in reversed(distances(count)):
        for j in list(got):
            got[j ^ distance] = swap(got[j], distance)
    return [got[j] for j in range(count)]


def scatter_rows(partial):
    count = lax.axis_size("tensor")
    held = {j: piece for j, piece in enumerate(partial)}
    for distance in distances(count):
        for j in [j for j in held if j & distance][::-1]:
            part = swap(held.pop(j).astype(jnp.bfloat16), distance)
            base = held[j ^ distance].astype(jnp.float32)
            held[j ^ distance] = base + part.astype(jnp.float32)
    return held[0].astype(jnp.float32)


def body(
    ids_beam,
    beam_map,
    lengths,
    embed_table,
    gain_attn,
    w_query,
    w_key,
    w_value,
    w_out,
    gain_mlp,
    w_gate,
    w_up,
    w_down,
    final_gain,
    score_weight,
):
    section, tensor = lax.axis_index("section"), lax.axis_index("tensor")
    sections, tensors = lax.axis_size("section"), lax.axis_size("tensor")
    batch, batches = lax.axis_index("batch"), lax.axis_size("batch")
    per_device, length = ids_beam.shape
    share = length // tensors
    slots = jnp.arange(tensors, dtype=jnp.int32) ^ tensor

    owned = batch * per_device + jnp.arange(per_device, dtype=jnp.int32)
    beams_owned = jnp.take(beam_map, owned)
    lengths_owned = jnp.take(lengths, owned)
    blocks = [ids_beam]
    for steps in range(1, batches):
        blocks.append(
            lax.ppermute(ids_beam, "batch", [(b, (b + steps) % batches) for b in range(batches)])
        )
    blocks = jnp.concatenate(blocks, axis=0)
    holder = (batch - beams_owned // per_device) % batches
    tokens = blocks[holder * per_device + beams_owned % per_device]

    cosine, sine = rope_tables(length)
    by_slot = lambda t: jnp.asarray(t.reshape(tensors, share, -1))[slots].reshape(length, -1)
    cosine, sine = by_slot(cosine), by_slot(sine)
    positions = (slots[:, None] * share + jnp.arange(share, dtype=jnp.int32)).reshape(length)
    tables = (cosine, sine, positions[:, None], positions[None, :])

    hidden, first = [], []
    for c in range(per_device):
        looked = jnp.take(embed_table, tokens[c], axis=0)
        columns = []
        for source in range(sections):
            pieces = []
            for j in range(tensors):
                if source == 0 and j == 0:
                    pieces.append(looked)
                    continue
                links = [(source * tensors + z, z ^ j) for z in range(tensors)]
                pieces.append(lax.ppermute(looked, BOTH, links))
            pieces = jnp.stack(pieces)
            columns += [
                lax.dynamic_index_in_dim(pieces, z ^ tensor, 0, False) for z in range(tensors)
            ]
        embedded = jnp.concatenate(columns, axis=1)
        normed = rms_norm(embedded, gain_attn)
        first.append(
            [lax.dynamic_slice_in_dim(normed, slots[j] * share, share, 0) for j in range(tensors)]
        )
        hidden.append(lax.dynamic_slice_in_dim(embedded, tensor * share, share, 0))

    for layer in range(sections):
        for c in range(per_device):
            if layer == 0:
                pieces = first[c]
            else:
                links = [(layer - 1, layer)]
                hidden[c] = lax.ppermute(hidden[c], "section", links)
                pieces = gather_rows(rms_norm(hidden[c], gain_attn))
            partial = fused(
                attention_kernel, "attention", tables, (w_query, w_key, w_value), w_out, pieces
            )
            attn_sum = scatter_rows(partial)
            middle = (hidden[c].astype(jnp.float32) + attn_sum).astype(jnp.bfloat16)
            pieces = gather_rows(rms_norm(middle, gain_mlp))
            partial = fused(mlp_kernel, "mlp", (), (w_gate, w_up), w_down, pieces)
            mlp_sum = scatter_rows(partial)
            hidden[c] = (middle.astype(jnp.float32) + mlp_sum).astype(jnp.bfloat16)

    finals = jnp.stack(hidden)
    last = sections - 1
    half = finals.shape[2] // sections
    shown = lax.dynamic_slice_in_dim(finals, section * half, half, 2)
    for target in range(last):
        part = lax.ppermute(
            finals[:, :, target * half : (target + 1) * half], "section", [(last, target)]
        )
        shown = jnp.where(section == target, part, shown)

    at = lengths_owned - 1 - tensor * share
    owner = (at >= 0) & (at < share) & (section == last)
    row = jnp.take_along_axis(finals, jnp.clip(at, 0, share - 1)[:, None, None], axis=1)
    values = row[:, 0].astype(jnp.float32)
    inverse = lax.rsqrt(jnp.mean(values * values, axis=-1, keepdims=True) + EPSILON)
    score = jnp.sum(
        values * inverse * final_gain.astype(jnp.float32) * score_weight.astype(jnp.float32),
        axis=-1,
    )
    score = jnp.where(owner, score, 0.0)
    devices = sections * tensors
    total = score
    for steps in range(1, devices):
        total = total + lax.ppermute(
            score, BOTH, [(d, (d + steps) % devices) for d in range(devices)]
        )
    return (shown, total)


def solution(mesh):
    placed = (
        P("batch", None),
        P(),
        P(),
        P(None, ("section", "tensor")),
        P("section", None),
        P("section", None, "tensor"),
        P("section", None, "tensor"),
        P("section", None, "tensor"),
        P("section", "tensor", None),
        P("section", None),
        P("section", None, "tensor"),
        P("section", None, "tensor"),
        P("section", "tensor", None),
        P(),
        P(),
    )
    return jax.shard_map(
        body,
        mesh=mesh,
        in_specs=placed,
        out_specs=(P("batch", "tensor", "section"), P("batch")),
        check_vma=False,
    )
```

```python
import functools

import jax
import jax.numpy as jnp
import numpy as np
from jax import lax
from jax.experimental import pallas as pl
from jax.experimental.pallas import tpu as pltpu
from jax.sharding import PartitionSpec as P

HEAD_DIM = 128
EPSILON = 1e-05
ROTARY_FREQ_BASE = 10000.0
BOTH = ("section", "tensor")
WIDE = 256
VMEM_LIMIT = 50 * 2**20


def rms_norm(hidden, scale_gain):
    values = hidden.astype(jnp.float32)
    inverse = lax.rsqrt(jnp.mean(values * values, axis=-1, keepdims=True) + EPSILON)
    return (values * inverse * scale_gain.astype(jnp.float32)).astype(jnp.bfloat16)


def rope_tables(length):
    half_dim = HEAD_DIM // 2
    frequency = ROTARY_FREQ_BASE ** (-(np.arange(half_dim, dtype=np.float64) / half_dim))
    angles = np.arange(length, dtype=np.float64)[:, None] * frequency[None, :]
    cosine, sine = np.cos(angles), np.sin(angles)
    cosine = np.concatenate([cosine, cosine], axis=1).astype(np.float32)
    sine = np.concatenate([-sine, sine], axis=1).astype(np.float32)
    return cosine, sine


def dot(left, right):
    return jnp.dot(left, right, preferred_element_type=jnp.float32)


def load_rows(x_refs, x_all):
    start = 0
    for ref in x_refs:
        x_all[start : start + ref.shape[0], :] = ref[...]
        start += ref.shape[0]


def add_part(part, total, out_refs):
    step = pl.program_id(0)

    @pl.when(step == 0)
    def _():
        total[...] = part

    @pl.when(step > 0)
    def _():
        total[...] += part

    @pl.when(step == pl.num_programs(0) - 1)
    def _():
        start = 0
        for ref in out_refs:
            ref[...] = total[start : start + ref.shape[0], :].astype(jnp.bfloat16)
            start += ref.shape[0]


def attention_kernel(count, cos_ref, sin_ref, row_ref, col_ref, wq_ref, wk_ref, wv_ref, wo_ref, *refs):
    x_refs, out_refs, (x_all, total) = refs[:count], refs[count:-2], refs[-2:]
    pl.when(pl.program_id(0) == 0)(lambda: load_rows(x_refs, x_all))
    x = x_all[...]
    cosine, sine = cos_ref[...], sin_ref[...]
    visible = row_ref[...] >= col_ref[...]
    query, key, value = dot(x, wq_ref[0]), dot(x, wk_ref[0]), dot(x, wv_ref[0])
    value = value.astype(jnp.bfloat16)
    outs = []
    for head in range(query.shape[1] // HEAD_DIM):
        cut = slice(head * HEAD_DIM, (head + 1) * HEAD_DIM)
        q, k, v = query[:, cut], key[:, cut], value[:, cut]
        q = (q * cosine + pltpu.roll(q, HEAD_DIM // 2, 1) * sine).astype(jnp.bfloat16)
        k = (k * cosine + pltpu.roll(k, HEAD_DIM // 2, 1) * sine).astype(jnp.bfloat16)
        scores = lax.dot_general(
            q, k, (((1,), (1,)), ((), ())), preferred_element_type=jnp.float32
        ) * HEAD_DIM ** (-0.5)
        scores = jnp.where(visible, scores, -jnp.inf)
        scores = jnp.exp(scores - jnp.max(scores, axis=-1, keepdims=True))
        probs = scores / jnp.sum(scores, axis=-1, keepdims=True)
        outs.append(dot(probs.astype(jnp.bfloat16), v).astype(jnp.bfloat16))
    add_part(dot(jnp.concatenate(outs, axis=1), wo_ref[0]), total, out_refs)


def mlp_kernel(count, wg_ref, wu_ref, wd_ref, *refs):
    x_refs, out_refs, (x_all, total) = refs[:count], refs[count:-2], refs[-2:]
    pl.when(pl.program_id(0) == 0)(lambda: load_rows(x_refs, x_all))
    x = x_all[...]
    gate, up = dot(x, wg_ref[0]), dot(x, wu_ref[0])
    inner = (gate / (1.0 + jnp.exp(-gate)) * up).astype(jnp.bfloat16)
    add_part(dot(inner, wd_ref[0]), total, out_refs)


def whole(array):
    return pl.BlockSpec(array.shape, lambda i: (0,) * array.ndim)


def fused(kernel, name, tables, by_columns, by_rows, pieces, cuts):
    width = pieces[0].shape[1]
    length = sum(piece.shape[0] for piece in pieces)
    hidden = by_rows.shape[1]
    wide = min(WIDE, hidden)
    weights = list(by_columns) + [by_rows]
    flops = 2 * length * sum(w.size for w in weights)
    traffic = 2 * sum(w.size for w in weights) + 4 * length * width
    return pl.pallas_call(
        functools.partial(kernel, len(pieces)),
        out_shape=[jax.ShapeDtypeStruct((rows, width), jnp.bfloat16) for rows in cuts],
        grid=(hidden // wide,),
        in_specs=[whole(t) for t in tables]
        + [pl.BlockSpec((1, width, wide), lambda i: (0, 0, i)) for _ in by_columns]
        + [pl.BlockSpec((1, wide, width), lambda i: (0, i, 0))]
        + [whole(p) for p in pieces],
        out_specs=[pl.BlockSpec((rows, width), lambda i: (0, 0)) for rows in cuts],
        scratch_shapes=[
            pltpu.VMEM((length, width), jnp.bfloat16),
            pltpu.VMEM((length, width), jnp.float32),
        ],
        compiler_params=pltpu.CompilerParams(
            dimension_semantics=("arbitrary",), vmem_limit_bytes=VMEM_LIMIT
        ),
        cost_estimate=pl.CostEstimate(flops=flops, bytes_accessed=traffic, transcendentals=0),
        name=name,
    )(*tables, *weights, *pieces)


def send(value, source, target, distance):
    count = lax.axis_size("tensor")
    links = [(source * count + z, target * count + (z ^ distance)) for z in range(count)]
    return lax.ppermute(value, BOTH, links)


def relayed(j):
    return j & (j - 1) != 0


def row_cuts(length):
    sections, tensors = lax.axis_size("section"), lax.axis_size("tensor")
    share = length // tensors
    cuts = []
    for j in range(tensors):
        cuts += [share] if relayed(j) else [share // sections] * sections
    return cuts


def gather_rows(own, layer):
    pieces = []
    for j in range(lax.axis_size("tensor")):
        for source in range(lax.axis_size("section")):
            local = j == 0 and source == layer
            pieces.append(own if local else send(own, source, layer, j))
    return pieces


def scatter_rows(partial, layer):
    sections, tensors = lax.axis_size("section"), lax.axis_size("tensor")
    partial = list(partial)
    held = {}
    for j in range(tensors):
        if relayed(j):
            held[j] = partial.pop(0)
        else:
            held[j] = [partial.pop(0) for _ in range(sections)]
    sums = jnp.where(lax.axis_index("section") == layer, held[0][layer], 0).astype(jnp.float32)
    arrived = []
    for bit in range(tensors.bit_length() - 1):
        distance = 1 << bit
        for j in [j for j in range(tensors - 1, 0, -1) if j in held and j & distance]:
            piece = held.pop(j)
            if relayed(j):
                part = send(piece.astype(jnp.bfloat16), layer, layer, distance)
                part = part.astype(jnp.float32)
                into = held[j ^ distance]
                if relayed(j ^ distance):
                    held[j ^ distance] = into.astype(jnp.float32) + part
                else:
                    rows = into[0].shape[0]
                    held[j ^ distance] = [
                        p.astype(jnp.float32) + part[h * rows : (h + 1) * rows]
                        for h, p in enumerate(into)
                    ]
            else:
                arrived += [
                    send(p.astype(jnp.bfloat16), layer, h, distance) for h, p in enumerate(piece)
                ]
    arrived += [send(held[0][h], layer, h, 0) for h in range(sections) if h != layer]
    for part in arrived:
        sums = sums + part.astype(jnp.float32)
    return sums


def layer_gains(gain):
    sections, section = lax.axis_size("section"), lax.axis_index("section")
    held = [gain]
    for steps in range(1, sections):
        links = [(h, (h + steps) % sections) for h in range(sections)]
        held.append(lax.ppermute(gain, "section", links))
    held = jnp.concatenate(held, axis=0)
    return [held[(section - layer) % sections] for layer in range(sections)]


def body(
    ids_beam,
    beam_map,
    lengths,
    embed_table,
    gain_attn,
    w_query,
    w_key,
    w_value,
    w_out,
    gain_mlp,
    w_gate,
    w_up,
    w_down,
    final_gain,
    score_weight,
):
    section, tensor = lax.axis_index("section"), lax.axis_index("tensor")
    sections, tensors = lax.axis_size("section"), lax.axis_size("tensor")
    batch, batches = lax.axis_index("batch"), lax.axis_size("batch")
    per_device, length = ids_beam.shape
    share = length // tensors
    slots = jnp.arange(tensors, dtype=jnp.int32) ^ tensor

    owned = batch * per_device + jnp.arange(per_device, dtype=jnp.int32)
    beams_owned = jnp.take(beam_map, owned)
    lengths_owned = jnp.take(lengths, owned)
    blocks = [ids_beam]
    for steps in range(1, batches):
        blocks.append(
            lax.ppermute(ids_beam, "batch", [(b, (b + steps) % batches) for b in range(batches)])
        )
    blocks = jnp.concatenate(blocks, axis=0)
    holder = (batch - beams_owned // per_device) % batches
    tokens = blocks[holder * per_device + beams_owned % per_device]

    cosine, sine = rope_tables(length)
    by_slot = lambda t: jnp.asarray(t.reshape(tensors, share, -1))[slots].reshape(length, -1)
    cosine, sine = by_slot(cosine), by_slot(sine)
    positions = (slots[:, None] * share + jnp.arange(share, dtype=jnp.int32)).reshape(length)
    tables = (cosine, sine, positions[:, None], positions[None, :])

    rows = share // sections
    cuts = row_cuts(length)
    gains_attn, gains_mlp = layer_gains(gain_attn), layer_gains(gain_mlp)
    hidden, first = [], []
    embedded = None
    for c in range(per_device):
        looked = jnp.take(embed_table, tokens[c], axis=0)
        if embedded is not None:
            looked, first[-1][0] = lax.optimization_barrier((looked, first[-1][0]))
        columns = []
        for source in range(sections):
            pieces = jnp.stack(
                [
                    looked if source == 0 and j == 0 else send(looked, source, 0, j)
                    for j in range(tensors)
                ]
            )
            columns += [
                lax.dynamic_index_in_dim(pieces, z ^ tensor, 0, False) for z in range(tensors)
            ]
        embedded = jnp.concatenate(columns, axis=1)
        normed = rms_norm(embedded, gains_attn[0])
        first.append(
            [lax.dynamic_slice_in_dim(normed, slots[j] * share, share, 0) for j in range(tensors)]
        )
        own = [
            lax.dynamic_slice_in_dim(embedded, tensor * share + h * rows, rows, 0)
            for h in range(sections)
        ]
        mine = own[0]
        for h in range(1, sections):
            mine = jnp.where(section == h, send(own[h], 0, h, 0), mine)
        hidden.append(mine)

    for layer in range(sections):
        for c in range(per_device):
            pieces = first[c] if layer == 0 else gather_rows(rms_norm(hidden[c], gains_attn[layer]), layer)
            partial = fused(
                attention_kernel,
                "attention",
                tables,
                (w_query, w_key, w_value),
                w_out,
                pieces,
                cuts,
            )
            attn_sum = scatter_rows(partial, layer)
            middle = (hidden[c].astype(jnp.float32) + attn_sum).astype(jnp.bfloat16)
            pieces = gather_rows(rms_norm(middle, gains_mlp[layer]), layer)
            partial = fused(mlp_kernel, "mlp", (), (w_gate, w_up), w_down, pieces, cuts)
            mlp_sum = scatter_rows(partial, layer)
            hidden[c] = (middle.astype(jnp.float32) + mlp_sum).astype(jnp.bfloat16)

    finals = jnp.stack(hidden)
    half = finals.shape[2] // sections
    shown = [lax.dynamic_slice_in_dim(finals, section * half, half, 2)]
    for steps in range(1, sections):
        part = lax.dynamic_slice_in_dim(finals, (section + steps) % sections * half, half, 2)
        links = [(h, (h + steps) % sections) for h in range(sections)]
        shown.append(lax.ppermute(part, "section", links))
    shown = jnp.stack([shown[k] for k in range(sections)])
    shown = jnp.concatenate(
        [
            lax.dynamic_index_in_dim(shown, (section - h) % sections, 0, False)
            for h in range(sections)
        ],
        axis=1,
    )

    at = lengths_owned - 1 - tensor * share - section * rows
    owner = (at >= 0) & (at < rows)
    row = jnp.take_along_axis(finals, jnp.clip(at, 0, rows - 1)[:, None, None], axis=1)
    values = row[:, 0].astype(jnp.float32)
    inverse = lax.rsqrt(jnp.mean(values * values, axis=-1, keepdims=True) + EPSILON)
    score = jnp.sum(
        values * inverse * final_gain.astype(jnp.float32) * score_weight.astype(jnp.float32),
        axis=-1,
    )
    score = jnp.where(owner, score, 0.0)
    devices = sections * tensors
    total = score
    for steps in range(1, devices):
        total = total + lax.ppermute(
            score, BOTH, [(d, (d + steps) % devices) for d in range(devices)]
        )
    return (shown, total)


def solution(mesh):
    placed = (
        P("batch", None),
        P(),
        P(),
        P(None, ("section", "tensor")),
        P("section", None),
        P("section", None, "tensor"),
        P("section", None, "tensor"),
        P("section", None, "tensor"),
        P("section", "tensor", None),
        P("section", None),
        P("section", None, "tensor"),
        P("section", None, "tensor"),
        P("section", "tensor", None),
        P(),
        P(),
    )
    return jax.shard_map(
        body,
        mesh=mesh,
        in_specs=placed,
        out_specs=(P("batch", "tensor", "section"), P("batch")),
        check_vma=False,
    )
```

```python
import functools

import jax
import jax.numpy as jnp
import numpy as np
from jax import lax
from jax.experimental import pallas as pl
from jax.experimental.pallas import tpu as pltpu
from jax.sharding import PartitionSpec as P

HEAD_DIM = 128
EPSILON = 1e-05
ROTARY_FREQ_BASE = 10000.0
BOTH = ("section", "tensor")
WIDE = 256
VMEM_LIMIT = 50 * 2**20


def rms_norm(hidden, scale_gain):
    values = hidden.astype(jnp.float32)
    inverse = lax.rsqrt(jnp.mean(values * values, axis=-1, keepdims=True) + EPSILON)
    return (values * inverse * scale_gain.astype(jnp.float32)).astype(jnp.bfloat16)


def rope_tables(length):
    half_dim = HEAD_DIM // 2
    frequency = ROTARY_FREQ_BASE ** (-(np.arange(half_dim, dtype=np.float64) / half_dim))
    angles = np.arange(length, dtype=np.float64)[:, None] * frequency[None, :]
    cosine, sine = np.cos(angles), np.sin(angles)
    cosine = np.concatenate([cosine, cosine], axis=1).astype(np.float32)
    sine = np.concatenate([-sine, sine], axis=1).astype(np.float32)
    return cosine, sine


def dot(left, right):
    return jnp.dot(left, right, preferred_element_type=jnp.float32)


def load_rows(x_refs, x_all):
    start = 0
    for ref in x_refs:
        x_all[start : start + ref.shape[0], :] = ref[...]
        start += ref.shape[0]


def add_part(part, total, out_refs):
    step = pl.program_id(0)

    @pl.when(step == 0)
    def _():
        total[...] = part

    @pl.when(step > 0)
    def _():
        total[...] += part

    @pl.when(step == pl.num_programs(0) - 1)
    def _():
        start = 0
        for ref in out_refs:
            ref[...] = total[start : start + ref.shape[0], :].astype(jnp.bfloat16)
            start += ref.shape[0]


def attention_kernel(count, cos_ref, sin_ref, row_ref, col_ref, wq_ref, wk_ref, wv_ref, wo_ref, *refs):
    x_refs, out_refs, (x_all, total) = refs[:count], refs[count:-2], refs[-2:]
    pl.when(pl.program_id(0) == 0)(lambda: load_rows(x_refs, x_all))
    x = x_all[...]
    cosine, sine = cos_ref[...], sin_ref[...]
    visible = row_ref[...] >= col_ref[...]
    query, key, value = dot(x, wq_ref[0]), dot(x, wk_ref[0]), dot(x, wv_ref[0])
    value = value.astype(jnp.bfloat16)
    outs = []
    for head in range(query.shape[1] // HEAD_DIM):
        cut = slice(head * HEAD_DIM, (head + 1) * HEAD_DIM)
        q, k, v = query[:, cut], key[:, cut], value[:, cut]
        q = (q * cosine + pltpu.roll(q, HEAD_DIM // 2, 1) * sine).astype(jnp.bfloat16)
        k = (k * cosine + pltpu.roll(k, HEAD_DIM // 2, 1) * sine).astype(jnp.bfloat16)
        scores = lax.dot_general(
            q, k, (((1,), (1,)), ((), ())), preferred_element_type=jnp.float32
        ) * HEAD_DIM ** (-0.5)
        scores = jnp.where(visible, scores, -jnp.inf)
        scores = jnp.exp(scores - jnp.max(scores, axis=-1, keepdims=True))
        probs = scores / jnp.sum(scores, axis=-1, keepdims=True)
        outs.append(dot(probs.astype(jnp.bfloat16), v).astype(jnp.bfloat16))
    add_part(dot(jnp.concatenate(outs, axis=1), wo_ref[0]), total, out_refs)


def mlp_kernel(count, wg_ref, wu_ref, wd_ref, *refs):
    x_refs, out_refs, (x_all, total) = refs[:count], refs[count:-2], refs[-2:]
    pl.when(pl.program_id(0) == 0)(lambda: load_rows(x_refs, x_all))
    x = x_all[...]
    gate, up = dot(x, wg_ref[0]), dot(x, wu_ref[0])
    inner = (gate / (1.0 + jnp.exp(-gate)) * up).astype(jnp.bfloat16)
    add_part(dot(inner, wd_ref[0]), total, out_refs)


def whole(array):
    return pl.BlockSpec(array.shape, lambda i: (0,) * array.ndim)


def fused(kernel, name, tables, by_columns, by_rows, pieces, cuts):
    width = pieces[0].shape[1]
    length = sum(piece.shape[0] for piece in pieces)
    hidden = by_rows.shape[1]
    wide = min(WIDE, hidden)
    weights = list(by_columns) + [by_rows]
    flops = 2 * length * sum(w.size for w in weights)
    traffic = 2 * sum(w.size for w in weights) + 4 * length * width
    return pl.pallas_call(
        functools.partial(kernel, len(pieces)),
        out_shape=[jax.ShapeDtypeStruct((rows, width), jnp.bfloat16) for rows in cuts],
        grid=(hidden // wide,),
        in_specs=[whole(t) for t in tables]
        + [pl.BlockSpec((1, width, wide), lambda i: (0, 0, i)) for _ in by_columns]
        + [pl.BlockSpec((1, wide, width), lambda i: (0, i, 0))]
        + [whole(p) for p in pieces],
        out_specs=[pl.BlockSpec((rows, width), lambda i: (0, 0)) for rows in cuts],
        scratch_shapes=[
            pltpu.VMEM((length, width), jnp.bfloat16),
            pltpu.VMEM((length, width), jnp.float32),
        ],
        compiler_params=pltpu.CompilerParams(
            dimension_semantics=("arbitrary",), vmem_limit_bytes=VMEM_LIMIT
        ),
        cost_estimate=pl.CostEstimate(flops=flops, bytes_accessed=traffic, transcendentals=0),
        name=name,
    )(*tables, *weights, *pieces)


def send(value, source, target, distance):
    count = lax.axis_size("tensor")
    links = [(source * count + z, target * count + (z ^ distance)) for z in range(count)]
    return lax.ppermute(value, BOTH, links)


def slot_order(count):
    bits = [1 << bit for bit in range(count.bit_length() - 1)]
    groups, left = [], list(range(count))
    for bit in bits[:-1]:
        groups.append([j for j in left if j & bit])
        left = [j for j in left if not j & bit]
    return groups, left


def row_cuts(length):
    sections, tensors = lax.axis_size("section"), lax.axis_size("tensor")
    share = length // tensors
    groups, left = slot_order(tensors)
    return [len(g) * share for g in groups] + [share // sections] * (sections * len(left))


def gather_rows(own, layer):
    groups, left = slot_order(lax.axis_size("tensor"))
    pieces = []
    for j in sum(groups, []) + left:
        for source in range(lax.axis_size("section")):
            local = j == 0 and source == layer
            pieces.append(own if local else send(own, source, layer, j))
    return pieces


def sum_nearby(partial, layer):
    sections, tensors = lax.axis_size("section"), lax.axis_size("tensor")
    groups, left = slot_order(tensors)
    rows = partial[-1].shape[0]
    held = {}
    for group, array in zip(groups, partial):
        for k, j in enumerate(group):
            for h in range(sections):
                start = (k * sections + h) * rows
                held[j, h] = (array, start)
    for k, j in enumerate(left):
        for h in range(sections):
            held[j, h] = (partial[len(groups) + k * sections + h], 0)
    value = lambda entry: entry[0][entry[1] : entry[1] + rows].astype(jnp.float32)
    for step, group in enumerate(groups):
        whole_group = held[group[0], 0][0]
        if whole_group.shape[0] != rows * sections * len(group):
            whole_group = jnp.concatenate(
                [value(held[j, h]) for j in group for h in range(sections)]
            ).astype(jnp.bfloat16)
        arrived = send(whole_group, layer, layer, 1 << step)
        for k, j in enumerate(group):
            for h in range(sections):
                start = (k * sections + h) * rows
                to = (j ^ (1 << step), h)
                held[to] = (value(held[to]) + value((arrived, start)), 0)
    return [[value(held[j, h]).astype(jnp.bfloat16) for h in range(sections)] for j in left]


def send_to_owners(nearby, layer):
    sections, tensors = lax.axis_size("section"), lax.axis_size("tensor")
    near, far = nearby if len(nearby) == 2 else (nearby[0], [])
    arrived = [send(piece, layer, h, tensors // 2) for h, piece in enumerate(far)]
    return arrived + [send(near[h], layer, h, 0) for h in range(sections) if h != layer]


def sum_arrived(nearby, arrived, layer):
    sums = jnp.where(lax.axis_index("section") == layer, nearby[0][layer], 0)
    sums = sums.astype(jnp.float32)
    for part in arrived:
        sums = sums + part.astype(jnp.float32)
    return sums


def after(values, *others):
    return lax.optimization_barrier((values, others))[0]


def layer_gains(gain):
    sections, section = lax.axis_size("section"), lax.axis_index("section")
    held = [gain]
    for steps in range(1, sections):
        links = [(h, (h + steps) % sections) for h in range(sections)]
        held.append(lax.ppermute(gain, "section", links))
    held = jnp.concatenate(held, axis=0)
    return [held[(section - layer) % sections] for layer in range(sections)]


def body(
    ids_beam,
    beam_map,
    lengths,
    embed_table,
    gain_attn,
    w_query,
    w_key,
    w_value,
    w_out,
    gain_mlp,
    w_gate,
    w_up,
    w_down,
    final_gain,
    score_weight,
):
    section, tensor = lax.axis_index("section"), lax.axis_index("tensor")
    sections, tensors = lax.axis_size("section"), lax.axis_size("tensor")
    batch, batches = lax.axis_index("batch"), lax.axis_size("batch")
    per_device, length = ids_beam.shape
    share = length // tensors

    owned = batch * per_device + jnp.arange(per_device, dtype=jnp.int32)
    beams_owned = jnp.take(beam_map, owned)
    lengths_owned = jnp.take(lengths, owned)
    blocks = [ids_beam]
    for steps in range(1, batches):
        blocks.append(
            lax.ppermute(ids_beam, "batch", [(b, (b + steps) % batches) for b in range(batches)])
        )
    blocks = jnp.concatenate(blocks, axis=0)
    holder = (batch - beams_owned // per_device) % batches
    tokens = blocks[holder * per_device + beams_owned % per_device]

    groups, left = slot_order(tensors)
    slots = jnp.asarray(sum(groups, []) + left, jnp.int32) ^ tensor
    cosine, sine = rope_tables(length)
    by_slot = lambda t: jnp.asarray(t.reshape(tensors, share, -1))[slots].reshape(length, -1)
    cosine, sine = by_slot(cosine), by_slot(sine)
    positions = (slots[:, None] * share + jnp.arange(share, dtype=jnp.int32)).reshape(length)
    tables = (cosine, sine, positions[:, None], positions[None, :])

    rows = share // sections
    cuts = row_cuts(length)
    gains_attn, gains_mlp = layer_gains(gain_attn), layer_gains(gain_mlp)

    def embed(looked):
        columns = []
        for source in range(sections):
            pieces = jnp.stack(
                [
                    looked if source == 0 and j == 0 else send(looked, source, 0, j)
                    for j in range(tensors)
                ]
            )
            columns += [
                lax.dynamic_index_in_dim(pieces, z ^ tensor, 0, False) for z in range(tensors)
            ]
        embedded = jnp.concatenate(columns, axis=1)
        normed = rms_norm(embedded, gains_attn[0])
        pieces = [
            lax.dynamic_slice_in_dim(normed, slots[j] * share, share, 0) for j in range(tensors)
        ]
        own = [
            lax.dynamic_slice_in_dim(embedded, tensor * share + h * rows, rows, 0)
            for h in range(sections)
        ]
        mine = own[0]
        for h in range(1, sections):
            mine = jnp.where(section == h, send(own[h], 0, h, 0), mine)
        return pieces, mine

    def compute(half, pieces):
        if half % 2:
            return fused(mlp_kernel, "mlp", (), (w_gate, w_up), w_down, pieces, cuts)
        weights = (w_query, w_key, w_value)
        return fused(attention_kernel, "attention", tables, weights, w_out, pieces, cuts)

    def add(base, sums):
        return (base.astype(jnp.float32) + sums).astype(jnp.bfloat16)

    halves = 2 * sections
    gains = [gains_attn[half // 2] if half % 2 == 0 else gains_mlp[half // 2] for half in range(halves)]
    looked = [jnp.take(embed_table, tokens[c], axis=0) for c in range(per_device)]
    hidden = [None] * per_device
    nearby = [None] * per_device
    arrived = [None] * per_device
    for half in range(halves):
        for c in range(per_device):
            if half == 0:
                if c:
                    looked[c] = after(looked[c], partial[-1])
                pieces, hidden[c] = embed(looked[c])
            else:
                if c or half > 1 or per_device > 1:
                    arrived[c] = after(arrived[c], partial[-1])
                hidden[c] = add(hidden[c], sum_arrived(nearby[c], arrived[c], (half - 1) // 2))
                pieces = gather_rows(rms_norm(hidden[c], gains[half]), half // 2)
            if half or c:
                before = (c - 1) % per_device
                pieces = after(pieces, nearby[before])
            partial = compute(half, pieces)
            nearby[c] = sum_nearby(partial, half // 2)
            arrived[c] = send_to_owners(nearby[c], half // 2)
    for c in range(per_device):
        hidden[c] = add(hidden[c], sum_arrived(nearby[c], arrived[c], sections - 1))

    finals = jnp.stack(hidden)
    half = finals.shape[2] // sections
    shown = [lax.dynamic_slice_in_dim(finals, section * half, half, 2)]
    for steps in range(1, sections):
        part = lax.dynamic_slice_in_dim(finals, (section + steps) % sections * half, half, 2)
        links = [(h, (h + steps) % sections) for h in range(sections)]
        shown.append(lax.ppermute(part, "section", links))
    shown = jnp.stack([shown[k] for k in range(sections)])
    shown = jnp.concatenate(
        [
            lax.dynamic_index_in_dim(shown, (section - h) % sections, 0, False)
            for h in range(sections)
        ],
        axis=1,
    )

    at = lengths_owned - 1 - tensor * share - section * rows
    owner = (at >= 0) & (at < rows)
    row = jnp.take_along_axis(finals, jnp.clip(at, 0, rows - 1)[:, None, None], axis=1)
    values = row[:, 0].astype(jnp.float32)
    inverse = lax.rsqrt(jnp.mean(values * values, axis=-1, keepdims=True) + EPSILON)
    score = jnp.sum(
        values * inverse * final_gain.astype(jnp.float32) * score_weight.astype(jnp.float32),
        axis=-1,
    )
    score = jnp.where(owner, score, 0.0)
    devices = sections * tensors
    total = score
    for steps in range(1, devices):
        total = total + lax.ppermute(
            score, BOTH, [(d, (d + steps) % devices) for d in range(devices)]
        )
    return (shown, total)


def solution(mesh):
    placed = (
        P("batch", None),
        P(),
        P(),
        P(None, ("section", "tensor")),
        P("section", None),
        P("section", None, "tensor"),
        P("section", None, "tensor"),
        P("section", None, "tensor"),
        P("section", "tensor", None),
        P("section", None),
        P("section", None, "tensor"),
        P("section", None, "tensor"),
        P("section", "tensor", None),
        P(),
        P(),
    )
    return jax.shard_map(
        body,
        mesh=mesh,
        in_specs=placed,
        out_specs=(P("batch", "tensor", "section"), P("batch")),
        check_vma=False,
    )
```

```python
import functools

import jax
import jax.numpy as jnp
import numpy as np
from jax import lax
from jax.experimental import pallas as pl
from jax.experimental.pallas import tpu as pltpu
from jax.sharding import PartitionSpec as P

HEAD_DIM = 128
EPSILON = 1e-05
ROTARY_FREQ_BASE = 10000.0
BOTH = ("section", "tensor")
WIDE = 256
OUT_WIDE = 1024
VMEM_LIMIT = 50 * 2**20


def rms_norm(hidden, scale_gain):
    values = hidden.astype(jnp.float32)
    inverse = lax.rsqrt(jnp.mean(values * values, axis=-1, keepdims=True) + EPSILON)
    return (values * inverse * scale_gain.astype(jnp.float32)).astype(jnp.bfloat16)


def rope_tables(length):
    half_dim = HEAD_DIM // 2
    frequency = ROTARY_FREQ_BASE ** (-(np.arange(half_dim, dtype=np.float64) / half_dim))
    angles = np.arange(length, dtype=np.float64)[:, None] * frequency[None, :]
    cosine, sine = np.cos(angles), np.sin(angles)
    cosine = np.concatenate([cosine, cosine], axis=1).astype(np.float32)
    sine = np.concatenate([-sine, sine], axis=1).astype(np.float32)
    return cosine, sine


def dot(left, right):
    return jnp.dot(left, right, preferred_element_type=jnp.float32)


def load_rows(x_refs, x_all):
    start = 0
    for ref in x_refs:
        x_all[start : start + ref.shape[0], :] = ref[...]
        start += ref.shape[0]


def attention_kernel(count, cos_ref, sin_ref, row_ref, col_ref, wq_ref, wk_ref, wv_ref, *refs):
    x_refs, (out_ref, x_all) = refs[:count], refs[count:]
    pl.when(pl.program_id(0) == 0)(lambda: load_rows(x_refs, x_all))
    x = x_all[...]
    cosine, sine = cos_ref[...], sin_ref[...]
    visible = row_ref[...] >= col_ref[...]
    query, key, value = dot(x, wq_ref[0]), dot(x, wk_ref[0]), dot(x, wv_ref[0])
    value = value.astype(jnp.bfloat16)
    for head in range(query.shape[1] // HEAD_DIM):
        cut = slice(head * HEAD_DIM, (head + 1) * HEAD_DIM)
        q, k, v = query[:, cut], key[:, cut], value[:, cut]
        q = (q * cosine + pltpu.roll(q, HEAD_DIM // 2, 1) * sine).astype(jnp.bfloat16)
        k = (k * cosine + pltpu.roll(k, HEAD_DIM // 2, 1) * sine).astype(jnp.bfloat16)
        scores = lax.dot_general(
            q, k, (((1,), (1,)), ((), ())), preferred_element_type=jnp.float32
        ) * HEAD_DIM ** (-0.5)
        scores = jnp.where(visible, scores, -jnp.inf)
        scores = jnp.exp(scores - jnp.max(scores, axis=-1, keepdims=True))
        probs = scores / jnp.sum(scores, axis=-1, keepdims=True)
        out_ref[:, cut] = dot(probs.astype(jnp.bfloat16), v).astype(jnp.bfloat16)


def gate_kernel(count, wg_ref, wu_ref, *refs):
    x_refs, (out_ref, x_all) = refs[:count], refs[count:]
    pl.when(pl.program_id(0) == 0)(lambda: load_rows(x_refs, x_all))
    x = x_all[...]
    gate, up = dot(x, wg_ref[0]), dot(x, wu_ref[0])
    out_ref[...] = (gate / (1.0 + jnp.exp(-gate)) * up).astype(jnp.bfloat16)


def down_kernel(x_ref, w_ref, *out_refs):
    part = dot(x_ref[...], w_ref[0]).astype(jnp.bfloat16)
    start = 0
    for ref in out_refs:
        ref[...] = part[start : start + ref.shape[0], :]
        start += ref.shape[0]


def whole(array):
    return pl.BlockSpec(array.shape, lambda i: (0,) * array.ndim)


def cost(length, weights, other):
    return pl.CostEstimate(
        flops=2 * length * sum(w.size for w in weights),
        bytes_accessed=2 * sum(w.size for w in weights) + other,
        transcendentals=0,
    )


def params():
    return pltpu.CompilerParams(
        dimension_semantics=("arbitrary",), vmem_limit_bytes=VMEM_LIMIT
    )


def inward(kernel, name, tables, weights, pieces):
    width = pieces[0].shape[1]
    length = sum(piece.shape[0] for piece in pieces)
    hidden = weights[0].shape[2]
    wide = min(WIDE, hidden)
    return pl.pallas_call(
        functools.partial(kernel, len(pieces)),
        out_shape=jax.ShapeDtypeStruct((length, hidden), jnp.bfloat16),
        grid=(hidden // wide,),
        in_specs=[whole(t) for t in tables]
        + [pl.BlockSpec((1, width, wide), lambda i: (0, 0, i)) for _ in weights]
        + [whole(p) for p in pieces],
        out_specs=pl.BlockSpec((length, wide), lambda i: (0, i)),
        scratch_shapes=[pltpu.VMEM((length, width), jnp.bfloat16)],
        compiler_params=params(),
        cost_estimate=cost(length, weights, 4 * length * width),
        name=name,
    )(*tables, *weights, *pieces)


def outward(name, inner, weight, cuts):
    length, hidden = inner.shape
    width = weight.shape[2]
    wide = min(OUT_WIDE, width)
    return pl.pallas_call(
        down_kernel,
        out_shape=[jax.ShapeDtypeStruct((rows, width), jnp.bfloat16) for rows in cuts],
        grid=(width // wide,),
        in_specs=[whole(inner), pl.BlockSpec((1, hidden, wide), lambda i: (0, 0, i))],
        out_specs=[pl.BlockSpec((rows, wide), lambda i: (0, i)) for rows in cuts],
        compiler_params=params(),
        cost_estimate=cost(length, [weight], 4 * length * width),
        name=name,
    )(inner, weight)


def send(value, source, target, distance):
    count = lax.axis_size("tensor")
    links = [(source * count + z, target * count + (z ^ distance)) for z in range(count)]
    return lax.ppermute(value, BOTH, links)


def slot_order(count):
    bits = [1 << bit for bit in range(count.bit_length() - 1)]
    groups, left = [], list(range(count))
    for bit in bits[:-1]:
        groups.append([j for j in left if j & bit])
        left = [j for j in left if not j & bit]
    return groups, left


def row_cuts(length):
    sections, tensors = lax.axis_size("section"), lax.axis_size("tensor")
    share = length // tensors
    groups, left = slot_order(tensors)
    return [len(g) * share for g in groups] + [share // sections] * (sections * len(left))


def gather_rows(own, layer):
    groups, left = slot_order(lax.axis_size("tensor"))
    pieces = []
    for j in sum(groups, []) + left:
        for source in range(lax.axis_size("section")):
            local = j == 0 and source == layer
            pieces.append(own if local else send(own, source, layer, j))
    return pieces


def sum_nearby(partial, layer):
    sections, tensors = lax.axis_size("section"), lax.axis_size("tensor")
    groups, left = slot_order(tensors)
    rows = partial[-1].shape[0]
    held = {}
    for group, array in zip(groups, partial):
        for k, j in enumerate(group):
            for h in range(sections):
                start = (k * sections + h) * rows
                held[j, h] = (array, start)
    for k, j in enumerate(left):
        for h in range(sections):
            held[j, h] = (partial[len(groups) + k * sections + h], 0)
    value = lambda entry: entry[0][entry[1] : entry[1] + rows].astype(jnp.float32)
    for step, group in enumerate(groups):
        whole_group = held[group[0], 0][0]
        if whole_group.shape[0] != rows * sections * len(group):
            whole_group = jnp.concatenate(
                [value(held[j, h]) for j in group for h in range(sections)]
            ).astype(jnp.bfloat16)
        arrived = send(whole_group, layer, layer, 1 << step)
        for k, j in enumerate(group):
            for h in range(sections):
                start = (k * sections + h) * rows
                to = (j ^ (1 << step), h)
                held[to] = (value(held[to]) + value((arrived, start)), 0)
    return [[value(held[j, h]).astype(jnp.bfloat16) for h in range(sections)] for j in left]


def send_to_owners(nearby, layer):
    sections, tensors = lax.axis_size("section"), lax.axis_size("tensor")
    near, far = nearby if len(nearby) == 2 else (nearby[0], [])
    arrived = [send(piece, layer, h, tensors // 2) for h, piece in enumerate(far)]
    return arrived + [send(near[h], layer, h, 0) for h in range(sections) if h != layer]


def sum_arrived(nearby, arrived, layer):
    sums = jnp.where(lax.axis_index("section") == layer, nearby[0][layer], 0)
    sums = sums.astype(jnp.float32)
    for part in arrived:
        sums = sums + part.astype(jnp.float32)
    return sums


def after(values, *others):
    return lax.optimization_barrier((values, others))[0]


def layer_gains(gain):
    sections, section = lax.axis_size("section"), lax.axis_index("section")
    held = [gain]
    for steps in range(1, sections):
        links = [(h, (h + steps) % sections) for h in range(sections)]
        held.append(lax.ppermute(gain, "section", links))
    held = jnp.concatenate(held, axis=0)
    return [held[(section - layer) % sections] for layer in range(sections)]


def body(
    ids_beam,
    beam_map,
    lengths,
    embed_table,
    gain_attn,
    w_query,
    w_key,
    w_value,
    w_out,
    gain_mlp,
    w_gate,
    w_up,
    w_down,
    final_gain,
    score_weight,
):
    section, tensor = lax.axis_index("section"), lax.axis_index("tensor")
    sections, tensors = lax.axis_size("section"), lax.axis_size("tensor")
    batch, batches = lax.axis_index("batch"), lax.axis_size("batch")
    per_device, length = ids_beam.shape
    share = length // tensors

    owned = batch * per_device + jnp.arange(per_device, dtype=jnp.int32)
    beams_owned = jnp.take(beam_map, owned)
    lengths_owned = jnp.take(lengths, owned)
    blocks = [ids_beam]
    for steps in range(1, batches):
        blocks.append(
            lax.ppermute(ids_beam, "batch", [(b, (b + steps) % batches) for b in range(batches)])
        )
    blocks = jnp.concatenate(blocks, axis=0)
    holder = (batch - beams_owned // per_device) % batches
    tokens = blocks[holder * per_device + beams_owned % per_device]

    groups, left = slot_order(tensors)
    slots = jnp.asarray(sum(groups, []) + left, jnp.int32) ^ tensor
    cosine, sine = rope_tables(length)
    by_slot = lambda t: jnp.asarray(t.reshape(tensors, share, -1))[slots].reshape(length, -1)
    cosine, sine = by_slot(cosine), by_slot(sine)
    positions = (slots[:, None] * share + jnp.arange(share, dtype=jnp.int32)).reshape(length)
    tables = (cosine, sine, positions[:, None], positions[None, :])

    rows = share // sections
    cuts = row_cuts(length)
    gains_attn, gains_mlp = layer_gains(gain_attn), layer_gains(gain_mlp)

    def embed(looked):
        columns = []
        for source in range(sections):
            pieces = jnp.stack(
                [
                    looked if source == 0 and j == 0 else send(looked, source, 0, j)
                    for j in range(tensors)
                ]
            )
            columns += [
                lax.dynamic_index_in_dim(pieces, z ^ tensor, 0, False) for z in range(tensors)
            ]
        embedded = jnp.concatenate(columns, axis=1)
        normed = rms_norm(embedded, gains_attn[0])
        pieces = [
            lax.dynamic_slice_in_dim(normed, slots[j] * share, share, 0) for j in range(tensors)
        ]
        own = [
            lax.dynamic_slice_in_dim(embedded, tensor * share + h * rows, rows, 0)
            for h in range(sections)
        ]
        mine = own[0]
        for h in range(1, sections):
            mine = jnp.where(section == h, send(own[h], 0, h, 0), mine)
        return pieces, mine

    def compute(half, pieces):
        if half % 2:
            inner = inward(gate_kernel, "gate", (), (w_gate, w_up), pieces)
            return outward("down", inner, w_down, cuts)
        weights = (w_query, w_key, w_value)
        inner = inward(attention_kernel, "attention", tables, weights, pieces)
        return outward("out", inner, w_out, cuts)

    def add(base, sums):
        return (base.astype(jnp.float32) + sums).astype(jnp.bfloat16)

    halves = 2 * sections
    gains = [gains_attn[half // 2] if half % 2 == 0 else gains_mlp[half // 2] for half in range(halves)]
    looked = [jnp.take(embed_table, tokens[c], axis=0) for c in range(per_device)]
    hidden = [None] * per_device
    nearby = [None] * per_device
    arrived = [None] * per_device
    for half in range(halves):
        for c in range(per_device):
            if half == 0:
                if c:
                    looked[c] = after(looked[c], pieces)
                pieces, hidden[c] = embed(looked[c])
            else:
                if c:
                    arrived[c] = after(arrived[c], normed)
                hidden[c] = add(hidden[c], sum_arrived(nearby[c], arrived[c], (half - 1) // 2))
                normed = rms_norm(hidden[c], gains[half])
                pieces = gather_rows(normed, half // 2)
            partial = compute(half, pieces)
            nearby[c] = sum_nearby(partial, half // 2)
            arrived[c] = send_to_owners(nearby[c], half // 2)
    for c in range(per_device):
        hidden[c] = add(hidden[c], sum_arrived(nearby[c], arrived[c], sections - 1))

    finals = jnp.stack(hidden)
    half = finals.shape[2] // sections
    shown = [lax.dynamic_slice_in_dim(finals, section * half, half, 2)]
    for steps in range(1, sections):
        part = lax.dynamic_slice_in_dim(finals, (section + steps) % sections * half, half, 2)
        links = [(h, (h + steps) % sections) for h in range(sections)]
        shown.append(lax.ppermute(part, "section", links))
    shown = jnp.stack([shown[k] for k in range(sections)])
    shown = jnp.concatenate(
        [
            lax.dynamic_index_in_dim(shown, (section - h) % sections, 0, False)
            for h in range(sections)
        ],
        axis=1,
    )

    at = lengths_owned - 1 - tensor * share - section * rows
    owner = (at >= 0) & (at < rows)
    row = jnp.take_along_axis(finals, jnp.clip(at, 0, rows - 1)[:, None, None], axis=1)
    values = row[:, 0].astype(jnp.float32)
    inverse = lax.rsqrt(jnp.mean(values * values, axis=-1, keepdims=True) + EPSILON)
    score = jnp.sum(
        values * inverse * final_gain.astype(jnp.float32) * score_weight.astype(jnp.float32),
        axis=-1,
    )
    score = jnp.where(owner, score, 0.0)
    devices = sections * tensors
    total = score
    for steps in range(1, devices):
        total = total + lax.ppermute(
            score, BOTH, [(d, (d + steps) % devices) for d in range(devices)]
        )
    return (shown, total)


def solution(mesh):
    placed = (
        P("batch", None),
        P(),
        P(),
        P(None, ("section", "tensor")),
        P("section", None),
        P("section", None, "tensor"),
        P("section", None, "tensor"),
        P("section", None, "tensor"),
        P("section", "tensor", None),
        P("section", None),
        P("section", None, "tensor"),
        P("section", None, "tensor"),
        P("section", "tensor", None),
        P(),
        P(),
    )
    return jax.shard_map(
        body,
        mesh=mesh,
        in_specs=placed,
        out_specs=(P("batch", "tensor", "section"), P("batch")),
        check_vma=False,
    )
```

```python
import functools

import jax
import jax.numpy as jnp
import numpy as np
from jax import lax
from jax.experimental import pallas as pl
from jax.experimental.pallas import tpu as pltpu
from jax.sharding import PartitionSpec as P

HEAD_DIM = 128
EPSILON = 1e-05
ROTARY_FREQ_BASE = 10000.0
BOTH = ("section", "tensor")
WIDE = 512
OUT_WIDE = 2048
VMEM_LIMIT = 50 * 2**20


def rms_norm(hidden, scale_gain):
    values = hidden.astype(jnp.float32)
    inverse = lax.rsqrt(jnp.mean(values * values, axis=-1, keepdims=True) + EPSILON)
    return (values * inverse * scale_gain.astype(jnp.float32)).astype(jnp.bfloat16)


def rope_tables(length):
    half_dim = HEAD_DIM // 2
    frequency = ROTARY_FREQ_BASE ** (-(np.arange(half_dim, dtype=np.float64) / half_dim))
    angles = np.arange(length, dtype=np.float64)[:, None] * frequency[None, :]
    cosine, sine = np.cos(angles), np.sin(angles)
    cosine = np.concatenate([cosine, cosine], axis=1).astype(np.float32)
    sine = np.concatenate([-sine, sine], axis=1).astype(np.float32)
    return cosine, sine


def dot(left, right):
    return jnp.dot(left, right, preferred_element_type=jnp.float32)


def load_rows(x_refs, x_all):
    start = 0
    for ref in x_refs:
        x_all[start : start + ref.shape[0], :] = ref[...]
        start += ref.shape[0]


def attention_kernel(count, cos_ref, sin_ref, row_ref, col_ref, wq_ref, wk_ref, wv_ref, *refs):
    x_refs, (out_ref, x_all) = refs[:count], refs[count:]
    pl.when(pl.program_id(0) == 0)(lambda: load_rows(x_refs, x_all))
    x = x_all[...]
    cosine, sine = cos_ref[...], sin_ref[...]
    visible = row_ref[...] >= col_ref[...]
    query, key, value = dot(x, wq_ref[0]), dot(x, wk_ref[0]), dot(x, wv_ref[0])
    value = value.astype(jnp.bfloat16)
    for head in range(query.shape[1] // HEAD_DIM):
        cut = slice(head * HEAD_DIM, (head + 1) * HEAD_DIM)
        q, k, v = query[:, cut], key[:, cut], value[:, cut]
        q = (q * cosine + pltpu.roll(q, HEAD_DIM // 2, 1) * sine).astype(jnp.bfloat16)
        k = (k * cosine + pltpu.roll(k, HEAD_DIM // 2, 1) * sine).astype(jnp.bfloat16)
        scores = lax.dot_general(
            q, k, (((1,), (1,)), ((), ())), preferred_element_type=jnp.float32
        ) * HEAD_DIM ** (-0.5)
        scores = jnp.where(visible, scores, -jnp.inf)
        scores = jnp.exp(scores - jnp.max(scores, axis=-1, keepdims=True))
        probs = scores / jnp.sum(scores, axis=-1, keepdims=True)
        out_ref[:, cut] = dot(probs.astype(jnp.bfloat16), v).astype(jnp.bfloat16)


def gate_kernel(count, wg_ref, wu_ref, *refs):
    x_refs, (out_ref, x_all) = refs[:count], refs[count:]
    pl.when(pl.program_id(0) == 0)(lambda: load_rows(x_refs, x_all))
    x = x_all[...]
    gate, up = dot(x, wg_ref[0]), dot(x, wu_ref[0])
    out_ref[...] = (gate / (1.0 + jnp.exp(-gate)) * up).astype(jnp.bfloat16)


def down_kernel(x_ref, w_ref, *out_refs):
    part = dot(x_ref[...], w_ref[0]).astype(jnp.bfloat16)
    start = 0
    for ref in out_refs:
        ref[...] = part[start : start + ref.shape[0], :]
        start += ref.shape[0]


def whole(array):
    return pl.BlockSpec(array.shape, lambda i: (0,) * array.ndim)


def cost(length, weights, other):
    return pl.CostEstimate(
        flops=2 * length * sum(w.size for w in weights),
        bytes_accessed=2 * sum(w.size for w in weights) + other,
        transcendentals=0,
    )


def params():
    return pltpu.CompilerParams(
        dimension_semantics=("arbitrary",), vmem_limit_bytes=VMEM_LIMIT
    )


def inward(kernel, name, tables, weights, pieces):
    width = pieces[0].shape[1]
    length = sum(piece.shape[0] for piece in pieces)
    hidden = weights[0].shape[2]
    wide = min(WIDE, hidden)
    return pl.pallas_call(
        functools.partial(kernel, len(pieces)),
        out_shape=jax.ShapeDtypeStruct((length, hidden), jnp.bfloat16),
        grid=(hidden // wide,),
        in_specs=[whole(t) for t in tables]
        + [pl.BlockSpec((1, width, wide), lambda i: (0, 0, i)) for _ in weights]
        + [whole(p) for p in pieces],
        out_specs=pl.BlockSpec((length, wide), lambda i: (0, i)),
        scratch_shapes=[pltpu.VMEM((length, width), jnp.bfloat16)],
        compiler_params=params(),
        cost_estimate=cost(length, weights, 4 * length * width),
        name=name,
    )(*tables, *weights, *pieces)


def outward(name, inner, weight, cuts):
    length, hidden = inner.shape
    width = weight.shape[2]
    wide = min(OUT_WIDE, width)
    return pl.pallas_call(
        down_kernel,
        out_shape=[jax.ShapeDtypeStruct((rows, width), jnp.bfloat16) for rows in cuts],
        grid=(width // wide,),
        in_specs=[whole(inner), pl.BlockSpec((1, hidden, wide), lambda i: (0, 0, i))],
        out_specs=[pl.BlockSpec((rows, wide), lambda i: (0, i)) for rows in cuts],
        compiler_params=params(),
        cost_estimate=cost(length, [weight], 4 * length * width),
        name=name,
    )(inner, weight)


def send(value, source, target, distance):
    count = lax.axis_size("tensor")
    links = [(source * count + z, target * count + (z ^ distance)) for z in range(count)]
    return lax.ppermute(value, BOTH, links)


def slot_order(count, direct=False):
    bits = [1 << bit for bit in range(count.bit_length() - 1)]
    groups, left = [], list(range(count))
    for bit in bits[:-1]:
        straight = [bit] if direct else []
        groups.append([j for j in left if j & bit and j not in straight])
        left = [j for j in left if not j & bit or j in straight]
    return groups, left


def row_cuts(length, direct=False):
    sections, tensors = lax.axis_size("section"), lax.axis_size("tensor")
    share = length // tensors
    groups, left = slot_order(tensors, direct)
    return [len(g) * share for g in groups] + [share // sections] * (sections * len(left))


def gather_rows(own, layer, direct=False):
    groups, left = slot_order(lax.axis_size("tensor"), direct)
    pieces = []
    for j in sum(groups, []) + left:
        for source in range(lax.axis_size("section")):
            local = j == 0 and source == layer
            pieces.append(own if local else send(own, source, layer, j))
    return pieces


def sum_nearby(partial, layer, direct=False):
    sections, tensors = lax.axis_size("section"), lax.axis_size("tensor")
    groups, left = slot_order(tensors, direct)
    rows = partial[-1].shape[0]
    held = {}
    for group, array in zip(groups, partial):
        for k, j in enumerate(group):
            for h in range(sections):
                start = (k * sections + h) * rows
                held[j, h] = (array, start)
    for k, j in enumerate(left):
        for h in range(sections):
            held[j, h] = (partial[len(groups) + k * sections + h], 0)
    value = lambda entry: entry[0][entry[1] : entry[1] + rows].astype(jnp.float32)
    for step, group in enumerate(groups):
        whole_group = held[group[0], 0][0]
        if whole_group.shape[0] != rows * sections * len(group):
            whole_group = jnp.concatenate(
                [value(held[j, h]) for j in group for h in range(sections)]
            ).astype(jnp.bfloat16)
        arrived = send(whole_group, layer, layer, 1 << step)
        for k, j in enumerate(group):
            for h in range(sections):
                start = (k * sections + h) * rows
                to = (j ^ (1 << step), h)
                held[to] = (value(held[to]) + value((arrived, start)), 0)
    return [[value(held[j, h]).astype(jnp.bfloat16) for h in range(sections)] for j in left]


def send_to_owners(nearby, layer, direct=False):
    sections, tensors = lax.axis_size("section"), lax.axis_size("tensor")
    return [
        send(piece, layer, h, j)
        for j, pieces in zip(slot_order(tensors, direct)[1], nearby)
        for h, piece in enumerate(pieces)
        if j or h != layer
    ]


def sum_arrived(nearby, arrived, layer):
    sums = jnp.where(lax.axis_index("section") == layer, nearby[0][layer], 0)
    sums = sums.astype(jnp.float32)
    for part in arrived:
        sums = sums + part.astype(jnp.float32)
    return sums


def after(values, *others):
    return lax.optimization_barrier((values, others))[0]


def layer_gains(gain):
    sections, section = lax.axis_size("section"), lax.axis_index("section")
    held = [gain]
    for steps in range(1, sections):
        links = [(h, (h + steps) % sections) for h in range(sections)]
        held.append(lax.ppermute(gain, "section", links))
    held = jnp.concatenate(held, axis=0)
    return [held[(section - layer) % sections] for layer in range(sections)]


def body(
    ids_beam,
    beam_map,
    lengths,
    embed_table,
    gain_attn,
    w_query,
    w_key,
    w_value,
    w_out,
    gain_mlp,
    w_gate,
    w_up,
    w_down,
    final_gain,
    score_weight,
):
    section, tensor = lax.axis_index("section"), lax.axis_index("tensor")
    sections, tensors = lax.axis_size("section"), lax.axis_size("tensor")
    batch, batches = lax.axis_index("batch"), lax.axis_size("batch")
    per_device, length = ids_beam.shape
    share = length // tensors

    owned = batch * per_device + jnp.arange(per_device, dtype=jnp.int32)
    beams_owned = jnp.take(beam_map, owned)
    lengths_owned = jnp.take(lengths, owned)
    blocks = [ids_beam]
    for steps in range(1, batches):
        blocks.append(
            lax.ppermute(ids_beam, "batch", [(b, (b + steps) % batches) for b in range(batches)])
        )
    blocks = jnp.concatenate(blocks, axis=0)
    holder = (batch - beams_owned // per_device) % batches
    tokens = blocks[holder * per_device + beams_owned % per_device]

    groups, left = slot_order(tensors)
    slots = jnp.asarray(sum(groups, []) + left, jnp.int32) ^ tensor
    cosine, sine = rope_tables(length)
    by_slot = lambda t: jnp.asarray(t.reshape(tensors, share, -1))[slots].reshape(length, -1)
    cosine, sine = by_slot(cosine), by_slot(sine)
    positions = (slots[:, None] * share + jnp.arange(share, dtype=jnp.int32)).reshape(length)
    tables = (cosine, sine, positions[:, None], positions[None, :])

    rows = share // sections
    gains_attn, gains_mlp = layer_gains(gain_attn), layer_gains(gain_mlp)

    def embed(looked):
        columns = []
        for source in range(sections):
            pieces = jnp.stack(
                [
                    looked if source == 0 and j == 0 else send(looked, source, 0, j)
                    for j in range(tensors)
                ]
            )
            columns += [
                lax.dynamic_index_in_dim(pieces, z ^ tensor, 0, False) for z in range(tensors)
            ]
        embedded = jnp.concatenate(columns, axis=1)
        normed = rms_norm(embedded, gains_attn[0])
        pieces = [
            lax.dynamic_slice_in_dim(normed, slots[j] * share, share, 0) for j in range(tensors)
        ]
        own = [
            lax.dynamic_slice_in_dim(embedded, tensor * share + h * rows, rows, 0)
            for h in range(sections)
        ]
        mine = own[0]
        for h in range(1, sections):
            mine = jnp.where(section == h, send(own[h], 0, h, 0), mine)
        return pieces, mine

    def compute(half, pieces, ready):
        cuts = row_cuts(length, half + 1 == halves)
        if half % 2:
            inner = inward(gate_kernel, "gate", (), (w_gate, w_up), pieces)
            inner = after(inner, ready) if ready else inner
            return outward("down", inner, w_down, cuts)
        weights = (w_query, w_key, w_value)
        inner = inward(attention_kernel, "attention", tables, weights, pieces)
        inner = after(inner, ready) if ready else inner
        return outward("out", inner, w_out, cuts)

    def add(base, sums):
        return (base.astype(jnp.float32) + sums).astype(jnp.bfloat16)

    halves = 2 * sections
    gains = [gains_attn[half // 2] if half % 2 == 0 else gains_mlp[half // 2] for half in range(halves)]
    looked = [jnp.take(embed_table, tokens[c], axis=0) for c in range(per_device)]
    hidden = [None] * per_device
    nearby = [None] * per_device
    arrived = [None] * per_device
    for half in range(halves):
        for c in range(per_device):
            if half == 0:
                if c:
                    looked[c] = after(looked[c], pieces)
                pieces, hidden[c] = embed(looked[c])
            else:
                if c:
                    arrived[c] = after(arrived[c], normed)
                hidden[c] = add(hidden[c], sum_arrived(nearby[c], arrived[c], (half - 1) // 2))
                normed = rms_norm(hidden[c], gains[half])
                pieces = gather_rows(normed, half // 2, half + 1 == halves)
            partial = compute(half, pieces, [hidden[c]] if half == 0 else [])
            nearby[c] = sum_nearby(partial, half // 2, half + 1 == halves)
            arrived[c] = send_to_owners(nearby[c], half // 2, half + 1 == halves)
    for c in range(per_device):
        hidden[c] = add(hidden[c], sum_arrived(nearby[c], arrived[c], sections - 1))

    finals = jnp.stack(hidden)
    half = finals.shape[2] // sections
    shown = [lax.dynamic_slice_in_dim(finals, section * half, half, 2)]
    for steps in range(1, sections):
        part = lax.dynamic_slice_in_dim(finals, (section + steps) % sections * half, half, 2)
        links = [(h, (h + steps) % sections) for h in range(sections)]
        shown.append(lax.ppermute(part, "section", links))
    shown = jnp.stack([shown[k] for k in range(sections)])
    shown = jnp.concatenate(
        [
            lax.dynamic_index_in_dim(shown, (section - h) % sections, 0, False)
            for h in range(sections)
        ],
        axis=1,
    )

    at = lengths_owned - 1 - tensor * share - section * rows
    owner = (at >= 0) & (at < rows)
    row = jnp.take_along_axis(finals, jnp.clip(at, 0, rows - 1)[:, None, None], axis=1)
    values = row[:, 0].astype(jnp.float32)
    inverse = lax.rsqrt(jnp.mean(values * values, axis=-1, keepdims=True) + EPSILON)
    score = jnp.sum(
        values * inverse * final_gain.astype(jnp.float32) * score_weight.astype(jnp.float32),
        axis=-1,
    )
    score = jnp.where(owner, score, 0.0)
    devices = sections * tensors
    total = score
    for steps in range(1, devices):
        total = total + lax.ppermute(
            score, BOTH, [(d, (d + steps) % devices) for d in range(devices)]
        )
    return (shown, total)


def solution(mesh):
    placed = (
        P("batch", None),
        P(),
        P(),
        P(None, ("section", "tensor")),
        P("section", None),
        P("section", None, "tensor"),
        P("section", None, "tensor"),
        P("section", None, "tensor"),
        P("section", "tensor", None),
        P("section", None),
        P("section", None, "tensor"),
        P("section", None, "tensor"),
        P("section", "tensor", None),
        P(),
        P(),
    )
    return jax.shard_map(
        body,
        mesh=mesh,
        in_specs=placed,
        out_specs=(P("batch", "tensor", "section"), P("batch")),
        check_vma=False,
    )
```

```python
import functools

import jax
import jax.numpy as jnp
import numpy as np
from jax import lax
from jax.experimental import pallas as pl
from jax.experimental.pallas import tpu as pltpu
from jax.sharding import PartitionSpec as P

HEAD_DIM = 128
EPSILON = 1e-05
ROTARY_FREQ_BASE = 10000.0
BOTH = ("section", "tensor")
WIDE = 256
OUT_WIDE = 1024
VMEM_LIMIT = 50 * 2**20


def rms_norm(hidden, scale_gain):
    values = hidden.astype(jnp.float32)
    inverse = lax.rsqrt(jnp.mean(values * values, axis=-1, keepdims=True) + EPSILON)
    return (values * inverse * scale_gain.astype(jnp.float32)).astype(jnp.bfloat16)


def rope_tables(length):
    half_dim = HEAD_DIM // 2
    frequency = ROTARY_FREQ_BASE ** (-(np.arange(half_dim, dtype=np.float64) / half_dim))
    angles = np.arange(length, dtype=np.float64)[:, None] * frequency[None, :]
    cosine, sine = np.cos(angles), np.sin(angles)
    cosine = np.concatenate([cosine, cosine], axis=1).astype(np.float32)
    sine = np.concatenate([-sine, sine], axis=1).astype(np.float32)
    return cosine, sine


def dot(left, right):
    return jnp.dot(left, right, preferred_element_type=jnp.float32)


def load_rows(x_refs, x_all):
    start = 0
    for ref in x_refs:
        x_all[start : start + ref.shape[0], :] = ref[...]
        start += ref.shape[0]


def attention_kernel(count, cos_ref, sin_ref, row_ref, col_ref, wq_ref, wk_ref, wv_ref, *refs):
    x_refs, (out_ref, x_all) = refs[:count], refs[count:]
    pl.when(pl.program_id(0) == 0)(lambda: load_rows(x_refs, x_all))
    x = x_all[...]
    cosine, sine = cos_ref[...], sin_ref[...]
    visible = row_ref[...] >= col_ref[...]
    query, key, value = dot(x, wq_ref[0]), dot(x, wk_ref[0]), dot(x, wv_ref[0])
    value = value.astype(jnp.bfloat16)
    for head in range(query.shape[1] // HEAD_DIM):
        cut = slice(head * HEAD_DIM, (head + 1) * HEAD_DIM)
        q, k, v = query[:, cut], key[:, cut], value[:, cut]
        q = (q * cosine + pltpu.roll(q, HEAD_DIM // 2, 1) * sine).astype(jnp.bfloat16)
        k = (k * cosine + pltpu.roll(k, HEAD_DIM // 2, 1) * sine).astype(jnp.bfloat16)
        scores = lax.dot_general(
            q, k, (((1,), (1,)), ((), ())), preferred_element_type=jnp.float32
        ) * HEAD_DIM ** (-0.5)
        scores = jnp.where(visible, scores, -jnp.inf)
        scores = jnp.exp(scores - jnp.max(scores, axis=-1, keepdims=True))
        probs = scores / jnp.sum(scores, axis=-1, keepdims=True)
        out_ref[:, cut] = dot(probs.astype(jnp.bfloat16), v).astype(jnp.bfloat16)


def gate_kernel(count, wg_ref, wu_ref, *refs):
    x_refs, (out_ref, x_all) = refs[:count], refs[count:]
    pl.when(pl.program_id(0) == 0)(lambda: load_rows(x_refs, x_all))
    x = x_all[...]
    gate, up = dot(x, wg_ref[0]), dot(x, wu_ref[0])
    out_ref[...] = (gate / (1.0 + jnp.exp(-gate)) * up).astype(jnp.bfloat16)


def down_kernel(x_ref, w_ref, *out_refs):
    part = dot(x_ref[...], w_ref[0]).astype(jnp.bfloat16)
    start = 0
    for ref in out_refs:
        ref[...] = part[start : start + ref.shape[0], :]
        start += ref.shape[0]


def whole(array):
    return pl.BlockSpec(array.shape, lambda i: (0,) * array.ndim)


def cost(length, weights, other):
    return pl.CostEstimate(
        flops=2 * length * sum(w.size for w in weights),
        bytes_accessed=2 * sum(w.size for w in weights) + other,
        transcendentals=0,
    )


def params():
    return pltpu.CompilerParams(
        dimension_semantics=("arbitrary",), vmem_limit_bytes=VMEM_LIMIT
    )


def inward(kernel, name, tables, weights, pieces):
    width = pieces[0].shape[1]
    length = sum(piece.shape[0] for piece in pieces)
    hidden = weights[0].shape[2]
    wide = min(WIDE, hidden)
    return pl.pallas_call(
        functools.partial(kernel, len(pieces)),
        out_shape=jax.ShapeDtypeStruct((length, hidden), jnp.bfloat16),
        grid=(hidden // wide,),
        in_specs=[whole(t) for t in tables]
        + [pl.BlockSpec((1, width, wide), lambda i: (0, 0, i)) for _ in weights]
        + [whole(p) for p in pieces],
        out_specs=pl.BlockSpec((length, wide), lambda i: (0, i)),
        scratch_shapes=[pltpu.VMEM((length, width), jnp.bfloat16)],
        compiler_params=params(),
        cost_estimate=cost(length, weights, 4 * length * width),
        name=name,
    )(*tables, *weights, *pieces)


def outward(name, inner, weight, cuts):
    length, hidden = inner.shape
    width = weight.shape[2]
    wide = min(OUT_WIDE, width)
    return pl.pallas_call(
        down_kernel,
        out_shape=[jax.ShapeDtypeStruct((rows, width), jnp.bfloat16) for rows in cuts],
        grid=(width // wide,),
        in_specs=[whole(inner), pl.BlockSpec((1, hidden, wide), lambda i: (0, 0, i))],
        out_specs=[pl.BlockSpec((rows, wide), lambda i: (0, i)) for rows in cuts],
        compiler_params=params(),
        cost_estimate=cost(length, [weight], 4 * length * width),
        name=name,
    )(inner, weight)


def send(value, source, target, distance):
    count = lax.axis_size("tensor")
    links = [(source * count + z, target * count + (z ^ distance)) for z in range(count)]
    return lax.ppermute(value, BOTH, links)


def slot_order(count):
    bits = [1 << bit for bit in range(count.bit_length() - 1)]
    groups, left = [], list(range(count))
    for bit in bits[:-1]:
        groups.append([j for j in left if j & bit])
        left = [j for j in left if not j & bit]
    return groups, left


def row_cuts(length):
    sections, tensors = lax.axis_size("section"), lax.axis_size("tensor")
    share = length // tensors
    groups, left = slot_order(tensors)
    return [len(g) * share for g in groups] + [share // sections] * (sections * len(left))


def gather_rows(own, layer):
    groups, left = slot_order(lax.axis_size("tensor"))
    pieces = []
    for j in sum(groups, []) + left:
        for source in range(lax.axis_size("section")):
            local = j == 0 and source == layer
            pieces.append(own if local else send(own, source, layer, j))
    return pieces


def sum_nearby(partial, layer):
    sections, tensors = lax.axis_size("section"), lax.axis_size("tensor")
    groups, left = slot_order(tensors)
    rows = partial[-1].shape[0]
    held = {}
    for group, array in zip(groups, partial):
        for k, j in enumerate(group):
            for h in range(sections):
                start = (k * sections + h) * rows
                held[j, h] = (array, start)
    for k, j in enumerate(left):
        for h in range(sections):
            held[j, h] = (partial[len(groups) + k * sections + h], 0)
    value = lambda entry: entry[0][entry[1] : entry[1] + rows].astype(jnp.float32)
    for step, group in enumerate(groups):
        whole_group = held[group[0], 0][0]
        if whole_group.shape[0] != rows * sections * len(group):
            whole_group = jnp.concatenate(
                [value(held[j, h]) for j in group for h in range(sections)]
            ).astype(jnp.bfloat16)
        arrived = send(whole_group, layer, layer, 1 << step)
        for k, j in enumerate(group):
            for h in range(sections):
                start = (k * sections + h) * rows
                to = (j ^ (1 << step), h)
                held[to] = (value(held[to]) + value((arrived, start)), 0)
    return [[value(held[j, h]).astype(jnp.bfloat16) for h in range(sections)] for j in left]


def send_to_owners(nearby, layer):
    sections, tensors = lax.axis_size("section"), lax.axis_size("tensor")
    near, far = nearby if len(nearby) == 2 else (nearby[0], [])
    arrived = [send(piece, layer, h, tensors // 2) for h, piece in enumerate(far)]
    return arrived + [send(near[h], layer, h, 0) for h in range(sections) if h != layer]


def sum_arrived(nearby, arrived, layer):
    sums = jnp.where(lax.axis_index("section") == layer, nearby[0][layer], 0)
    sums = sums.astype(jnp.float32)
    for part in arrived:
        sums = sums + part.astype(jnp.float32)
    return sums


def after(values, *others):
    return lax.optimization_barrier((values, others))[0]


def layer_gains(gain):
    sections, section = lax.axis_size("section"), lax.axis_index("section")
    held = [gain]
    for steps in range(1, sections):
        links = [(h, (h + steps) % sections) for h in range(sections)]
        held.append(lax.ppermute(gain, "section", links))
    held = jnp.concatenate(held, axis=0)
    return [held[(section - layer) % sections] for layer in range(sections)]


def body(
    ids_beam,
    beam_map,
    lengths,
    embed_table,
    gain_attn,
    w_query,
    w_key,
    w_value,
    w_out,
    gain_mlp,
    w_gate,
    w_up,
    w_down,
    final_gain,
    score_weight,
):
    section, tensor = lax.axis_index("section"), lax.axis_index("tensor")
    sections, tensors = lax.axis_size("section"), lax.axis_size("tensor")
    batch, batches = lax.axis_index("batch"), lax.axis_size("batch")
    per_device, length = ids_beam.shape
    share = length // tensors

    owned = batch * per_device + jnp.arange(per_device, dtype=jnp.int32)
    beams_owned = jnp.take(beam_map, owned)
    lengths_owned = jnp.take(lengths, owned)
    blocks = [ids_beam]
    for steps in range(1, batches):
        blocks.append(
            lax.ppermute(ids_beam, "batch", [(b, (b + steps) % batches) for b in range(batches)])
        )
    blocks = jnp.concatenate(blocks, axis=0)
    holder = (batch - beams_owned // per_device) % batches
    tokens = blocks[holder * per_device + beams_owned % per_device]

    groups, left = slot_order(tensors)
    slots = jnp.asarray(sum(groups, []) + left, jnp.int32) ^ tensor
    cosine, sine = rope_tables(length)
    by_slot = lambda t: jnp.asarray(t.reshape(tensors, share, -1))[slots].reshape(length, -1)
    cosine, sine = by_slot(cosine), by_slot(sine)
    positions = (slots[:, None] * share + jnp.arange(share, dtype=jnp.int32)).reshape(length)
    tables = (cosine, sine, positions[:, None], positions[None, :])

    rows = share // sections
    cuts = row_cuts(length)
    gains_attn, gains_mlp = layer_gains(gain_attn), layer_gains(gain_mlp)

    def embed(looked):
        columns = []
        for source in range(sections):
            pieces = jnp.stack(
                [
                    looked if source == 0 and j == 0 else send(looked, source, 0, j)
                    for j in range(tensors)
                ]
            )
            columns += [
                lax.dynamic_index_in_dim(pieces, z ^ tensor, 0, False) for z in range(tensors)
            ]
        embedded = jnp.concatenate(columns, axis=1)
        normed = rms_norm(embedded, gains_attn[0])
        pieces = [
            lax.dynamic_slice_in_dim(normed, slots[j] * share, share, 0) for j in range(tensors)
        ]
        own = [
            lax.dynamic_slice_in_dim(embedded, tensor * share + h * rows, rows, 0)
            for h in range(sections)
        ]
        mine = own[0]
        for h in range(1, sections):
            mine = jnp.where(section == h, send(own[h], 0, h, 0), mine)
        return pieces, mine

    def compute(half, pieces, ready):
        if half % 2:
            inner = inward(gate_kernel, "gate", (), (w_gate, w_up), pieces)
            inner = after(inner, ready) if ready else inner
            return outward("down", inner, w_down, cuts)
        weights = (w_query, w_key, w_value)
        inner = inward(attention_kernel, "attention", tables, weights, pieces)
        inner = after(inner, ready) if ready else inner
        return outward("out", inner, w_out, cuts)

    def add(base, sums):
        return (base.astype(jnp.float32) + sums).astype(jnp.bfloat16)

    halves = 2 * sections
    gains = [gains_attn[half // 2] if half % 2 == 0 else gains_mlp[half // 2] for half in range(halves)]
    looked = [jnp.take(embed_table, tokens[c], axis=0) for c in range(per_device)]
    hidden = [None] * per_device
    nearby = [None] * per_device
    arrived = [None] * per_device
    for half in range(halves):
        for c in range(per_device):
            if half == 0:
                if c:
                    looked[c] = after(looked[c], pieces)
                pieces, hidden[c] = embed(looked[c])
            else:
                if c:
                    arrived[c] = after(arrived[c], normed)
                hidden[c] = add(hidden[c], sum_arrived(nearby[c], arrived[c], (half - 1) // 2))
                normed = rms_norm(hidden[c], gains[half])
                pieces = gather_rows(normed, half // 2)
            partial = compute(half, pieces, [hidden[c]] if half == 0 else [])
            nearby[c] = sum_nearby(partial, half // 2)
            arrived[c] = send_to_owners(nearby[c], half // 2)
    for c in range(per_device):
        hidden[c] = add(hidden[c], sum_arrived(nearby[c], arrived[c], sections - 1))

    finals = jnp.stack(hidden)
    half = finals.shape[2] // sections
    shown = [lax.dynamic_slice_in_dim(finals, section * half, half, 2)]
    for steps in range(1, sections):
        part = lax.dynamic_slice_in_dim(finals, (section + steps) % sections * half, half, 2)
        links = [(h, (h + steps) % sections) for h in range(sections)]
        shown.append(lax.ppermute(part, "section", links))
    shown = jnp.stack([shown[k] for k in range(sections)])
    shown = jnp.concatenate(
        [
            lax.dynamic_index_in_dim(shown, (section - h) % sections, 0, False)
            for h in range(sections)
        ],
        axis=1,
    )

    at = lengths_owned - 1 - tensor * share - section * rows
    owner = (at >= 0) & (at < rows)
    row = jnp.take_along_axis(finals, jnp.clip(at, 0, rows - 1)[:, None, None], axis=1)
    values = row[:, 0].astype(jnp.float32)
    inverse = lax.rsqrt(jnp.mean(values * values, axis=-1, keepdims=True) + EPSILON)
    score = jnp.sum(
        values * inverse * final_gain.astype(jnp.float32) * score_weight.astype(jnp.float32),
        axis=-1,
    )
    score = jnp.where(owner, score, 0.0)
    devices = sections * tensors
    total = score
    for steps in range(1, devices):
        total = total + lax.ppermute(
            score, BOTH, [(d, (d + steps) % devices) for d in range(devices)]
        )
    return (shown, total)


def solution(mesh):
    placed = (
        P("batch", None),
        P(),
        P(),
        P(None, ("section", "tensor")),
        P("section", None),
        P("section", None, "tensor"),
        P("section", None, "tensor"),
        P("section", None, "tensor"),
        P("section", "tensor", None),
        P("section", None),
        P("section", None, "tensor"),
        P("section", None, "tensor"),
        P("section", "tensor", None),
        P(),
        P(),
    )
    return jax.shard_map(
        body,
        mesh=mesh,
        in_specs=placed,
        out_specs=(P("batch", "tensor", "section"), P("batch")),
        check_vma=False,
    )
```
